32 devices in a mesh: swap: 4 (over x, core), regroup: 8 (over z, y).
Axes of the slice: x: 2, y: 2, z: 4, core: 2. Of those that a mesh axis runs over, the one named last changes fastest.
Arguments:
- state: float32 [2, 16384, 128], P(None, ('swap', 'regroup')), may hold values from -6 to 6
- gates: float32 [2, 12, 128, 128], replicated, may hold values from -0.375 to 0.375
- control_bits: int32 [12, 2], replicated, may hold values from 0 to 8
- patterns: int32 [12], replicated, may hold values from 0 to 65535
- swap_qubits: int32 [3], replicated, may hold values from 0 to 8
Outputs:
- final_state: float32 [2, 16384, 128], P(None, ('swap', 'regroup'))
The draws below stay inside these ranges and needn't reach their ends.
All inputs are finite; a program needn't handle non-finite values.
Results may differ from the reference program's by a relative error of at most 0.0001.
Values sent between devices are 32-bit elements; how exact they have to be, the bound alone decides.
No kernel may reach another device: no remote copies, remote signals or barrier semaphores. Data moves between devices by JAX's collectives and lax.ppermute only.
A program may use at most 64 MiB of HBM per device.

```python
import jax
import jax.numpy as jnp
from jax import lax

ROW_BITS = 9
SWAPS = 3
BLOCK = 128
GATES = 12
ROWS = 16384
N_SWAP = 4
N_REGROUP = 8


def set_ends(entries, stream_key, low, top_value):
    dims = entries.shape
    spot = [jax.random.randint(jax.random.fold_in(stream_key, axis), (), 0, dims[axis]) for axis in range(len(dims))]
    entries = entries.at[tuple(spot)].set(low)
    longest = dims.index(max(dims))
    spot[longest] = (spot[longest] + 1) % dims[longest]
    return entries.at[tuple(spot)].set(top_value)


def shard_levels(rng, shape, pieces, smallest, high):
    loudness, own = 1.0, jax.random.fold_in(rng, 6)
    for axis_at, shards_of in pieces:
        steps = jnp.exp(jax.random.uniform(jax.random.fold_in(own, axis_at), (shards_of,), jnp.float32, smallest / len(pieces), high / len(pieces)))
        loudness = loudness * jnp.repeat(steps, shape[axis_at] // shards_of).reshape([-1 if axis == axis_at else 1 for axis in range(len(shape))])
    return loudness


def normal_values(rng, shape, deviation, reach, cuts=(), held_as=jnp.bfloat16):
    values = deviation * jax.random.normal(rng, shape, jnp.float32)
    if cuts:
        values = values * shard_levels(rng, shape, cuts, -0.22, 0.18)
    return jnp.clip(values, -reach, reach).astype(held_as)


def setup_inputs(seed: int = 0) -> dict:
    seeds = jax.random.split(jax.random.key(seed), 6)
    return {
        "state": normal_values(seeds[0], (2, ROWS, BLOCK), 1.0, 6.0, ((1, 32),), jnp.float32),
        "gates": normal_values(seeds[1], (2, GATES, BLOCK, BLOCK), (2 * BLOCK) ** -0.5, 0.375, (), jnp.float32),
        "control_bits": set_ends(jax.random.randint(seeds[2], (GATES, 2), 0, ROW_BITS), jax.random.fold_in(seeds[2], 1), 0, ROW_BITS - 1).astype(jnp.int32),
        "patterns": set_ends(jax.random.randint(seeds[3], (GATES,), 0, 65536), jax.random.fold_in(seeds[3], 1), 0, 65535).astype(jnp.int32),
        "swap_qubits": jax.random.randint(seeds[4], (SWAPS,), 0, ROW_BITS).astype(jnp.int32),
    }


def complex_product(real_part, imag_part, matrix):
    highest = lax.Precision.HIGHEST
    mat_real = matrix[0].T
    mat_imag = matrix[1].T
    new_real = jnp.dot(real_part, mat_real, precision=highest) - jnp.dot(imag_part, mat_imag, precision=highest)
    new_imag = jnp.dot(real_part, mat_imag, precision=highest) + jnp.dot(imag_part, mat_real, precision=highest)
    return new_real, new_imag


def target_active(columns, pattern):
    groups = lax.broadcasted_iota(jnp.int32, (columns,), 0) // (columns // 16)
    return jnp.bitwise_and(jnp.right_shift(pattern, groups), 1) == 1


def apply_gate(amplitudes, row_ids, matrix, control_mask, pattern):
    real_part = amplitudes[0]
    imag_part = amplitudes[1]
    new_real, new_imag = complex_product(real_part, imag_part, matrix)
    col_on = target_active(real_part.shape[-1], pattern)
    row_on = jnp.bitwise_and(row_ids, control_mask) == control_mask
    active = jnp.logical_and(row_on[..., None], col_on)
    return jnp.stack([jnp.where(active, new_real, real_part), jnp.where(active, new_imag, imag_part)])


def apply_pair_gate(amplitudes, row_count, matrix, control_mask, pattern, qubit):
    rows_all = amplitudes.shape[1]
    columns = amplitudes.shape[2]
    half_rows = rows_all // 2
    half_cols = columns // 2
    one = jnp.int32(1)
    offsets = lax.iota(jnp.int32, half_rows)
    low_bits = jnp.bitwise_and(offsets, jnp.left_shift(one, qubit) - 1)
    high_bits = jnp.left_shift(jnp.right_shift(offsets, qubit), qubit + 1)
    zero_rows = jnp.bitwise_or(high_bits, low_bits)
    one_rows = jnp.bitwise_or(zero_rows, jnp.left_shift(one, qubit))
    lower_rows = jnp.take(amplitudes, zero_rows, axis=1).reshape(2, half_rows, 2, half_cols)
    upper_rows = jnp.take(amplitudes, one_rows, axis=1).reshape(2, half_rows, 2, half_cols)
    joined = jnp.concatenate([lower_rows, upper_rows], axis=3)
    flat_real = joined[0].reshape(half_rows * 2, columns)
    flat_imag = joined[1].reshape(half_rows * 2, columns)
    new_real, new_imag = complex_product(flat_real, flat_imag, matrix)
    new_real = new_real.reshape(half_rows, 2, columns)
    new_imag = new_imag.reshape(half_rows, 2, columns)
    cleared = jnp.bitwise_and(control_mask, jnp.bitwise_not(jnp.left_shift(one, qubit)))
    local_ids = jnp.bitwise_and(zero_rows, row_count - 1)
    row_on = jnp.bitwise_and(local_ids, cleared) == cleared
    col_on = target_active(columns, pattern)
    active = jnp.logical_and(row_on[:, None, None], col_on)
    merged = jnp.stack([jnp.where(active, new_real, joined[0]), jnp.where(active, new_imag, joined[1])])
    new_lower = merged[..., :half_cols].reshape(2, half_rows, columns)
    new_upper = merged[..., half_cols:].reshape(2, half_rows, columns)
    return amplitudes.at[:, zero_rows].set(new_lower).at[:, one_rows].set(new_upper)


def reference(state, gates, control_bits, patterns, swap_qubits):
    rows_all = state.shape[1]
    row_count = 2 ** ROW_BITS
    row_index = lax.iota(jnp.int32, rows_all)
    local_rows = jnp.bitwise_and(row_index, row_count - 1)
    one = jnp.int32(1)
    control_masks = jnp.bitwise_or(jnp.left_shift(one, control_bits[:, 0]), jnp.left_shift(one, control_bits[:, 1]))
    reg_levels = N_REGROUP.bit_length() - 1
    swap_levels = N_SWAP.bit_length() - 1
    current = state
    for gate_num in range(3 * (SWAPS + 1)):
        if gate_num % 3 == 1 and gate_num >= 4:
            qubit = swap_qubits[(gate_num - 4) // 3]
            current = apply_pair_gate(current, row_count, gates[:, gate_num], control_masks[gate_num], patterns[gate_num], qubit)
        else:
            current = apply_gate(current, local_rows, gates[:, gate_num], control_masks[gate_num], patterns[gate_num])
        swap_turn = gate_num // 3
        if gate_num % 3 == 2 and swap_turn < SWAPS:
            high_bit = ROW_BITS + reg_levels + swap_turn % swap_levels
            local_qubit = swap_qubits[swap_turn]
            differ = jnp.bitwise_and(jnp.bitwise_xor(jnp.right_shift(row_index, high_bit), jnp.right_shift(row_index, local_qubit)), 1)
            source = jnp.bitwise_xor(jnp.bitwise_xor(row_index, jnp.left_shift(differ, high_bit)), jnp.left_shift(differ, local_qubit))
            current = jnp.take(current, source, axis=1)
    columns = state.shape[2]
    piece_rows = row_count // N_REGROUP
    shaped = current.reshape(2, N_SWAP, N_REGROUP, N_REGROUP, piece_rows, columns)
    return jnp.swapaxes(shaped, 2, 3).reshape(2, rows_all, columns)
```

```python
import jax
import jax.numpy as jnp
from jax import lax
from jax.experimental import pallas as pl
from jax.experimental.pallas import tpu as pltpu
from jax.sharding import PartitionSpec as P


SWAPS = 3
TILE = 8
VMEM = pltpu.VMEM
SMEM = pltpu.SMEM


def in_vmem(count):
    return [pl.BlockSpec(memory_space=VMEM) for _ in range(count)]


def in_smem(count):
    return [pl.BlockSpec(memory_space=SMEM) for _ in range(count)]


def prepare_kernel(gates, high, low):
    order = gates.shape[-1]
    for gate in range(gates.shape[1]):
        real = gates[0, gate]
        imag = gates[1, gate]

        def put(rows, cols, value):
            top = value.astype(jnp.bfloat16)
            high[gate, rows : rows + order, cols : cols + order] = top
            low[gate, rows : rows + order, cols : cols + order] = (value - top.astype(jnp.float32)).astype(jnp.bfloat16)

        put(0, 0, real)
        put(0, order, -imag)
        put(order, 0, imag)
        put(order, order, real)


def prepare(gates):
    count, order = gates.shape[1], gates.shape[2]
    shape = jax.ShapeDtypeStruct((count, 2 * order, 2 * order), jnp.bfloat16)
    return pl.pallas_call(
        prepare_kernel, out_shape=(shape, shape), in_specs=in_vmem(1), out_specs=tuple(in_vmem(2)), name="prepare"
    )(gates)


def times(left, right):
    return lax.dot_general(left, right, (((1,), (1,)), ((), ())), preferred_element_type=jnp.float32)


def plain_gate(state, gate, high, low, row_mask, pattern, chunk):
    rows_all, columns = state.shape[1], state.shape[2]
    lanes = lax.broadcasted_iota(jnp.int32, (chunk, columns), 1)
    rows = lax.broadcasted_iota(jnp.int32, (chunk, columns), 0)
    col_on = ((pattern >> (lanes // (columns // 16))) & 1) == 1
    matrix_high = high[gate]
    matrix_low = low[gate]
    for start in range(0, rows_all, chunk):
        real = state[0, start : start + chunk, :]
        imag = state[1, start : start + chunk, :]
        both = jnp.concatenate([real, imag], axis=1)
        both_high = both.astype(jnp.bfloat16)
        both_low = (both - both_high.astype(jnp.float32)).astype(jnp.bfloat16)
        new = times(both_high, matrix_high) + times(both_low, matrix_high) + times(both_high, matrix_low)
        on = (((rows + start) & row_mask) == row_mask) & col_on
        state[0, start : start + chunk, :] = jnp.where(on, new[:, :columns], real)
        state[1, start : start + chunk, :] = jnp.where(on, new[:, columns:], imag)


def insert_bit(index, bit, value):
    low = index & ((1 << bit) - 1)
    return ((index >> bit) << (bit + 1)) | low | (value << bit)


def exchange_column_bit(state, qubit):
    rows_all, columns = state.shape[1], state.shape[2]
    half = columns // 2
    lane_low = lax.broadcasted_iota(jnp.int32, (TILE, columns), 1) < half
    sub = lax.broadcasted_iota(jnp.int32, (TILE, columns), 0)
    tiles = rows_all // TILE

    @pl.when(qubit >= 3)
    def _():
        bit = qubit - 3

        def step(k, carry):
            first = pl.multiple_of(insert_bit(k, bit, 0) * TILE, TILE)
            second = pl.multiple_of(insert_bit(k, bit, 1) * TILE, TILE)
            for plane in range(2):
                a = state[plane, pl.ds(first, TILE), :]
                b = state[plane, pl.ds(second, TILE), :]
                state[plane, pl.ds(first, TILE), :] = jnp.where(lane_low, a, pltpu.roll(b, half, 1))
                state[plane, pl.ds(second, TILE), :] = jnp.where(lane_low, pltpu.roll(a, half, 1), b)
            return carry

        lax.fori_loop(0, tiles // 2, step, 0, unroll=8)

    for low_bit in range(3):

        @pl.when(qubit == low_bit)
        def _():
            distance = 1 << low_bit
            zero = ((sub >> low_bit) & 1) == 0
            keep = zero == lane_low

            def step(k, carry):
                at = pl.multiple_of(k * TILE, TILE)
                for plane in range(2):
                    a = state[plane, pl.ds(at, TILE), :]
                    turned = pltpu.roll(a, half, 1)
                    partner = jnp.where(zero, pltpu.roll(turned, TILE - distance, 0), pltpu.roll(turned, distance, 0))
                    state[plane, pl.ds(at, TILE), :] = jnp.where(keep, a, partner)
                return carry

            lax.fori_loop(0, tiles, step, 0, unroll=8)


def take_out(state, sent, qubit, value):
    columns = state.shape[2]
    tiles = sent.shape[1] // TILE
    sub = lax.broadcasted_iota(jnp.int32, (TILE, columns), 0)

    @pl.when(qubit >= 3)
    def _():
        def step(k, carry):
            at = pl.multiple_of(insert_bit(k, qubit - 3, value) * TILE, TILE)
            for plane in range(2):
                sent[plane, pl.ds(pl.multiple_of(k * TILE, TILE), TILE), :] = state[plane, pl.ds(at, TILE), :]
            return carry

        lax.fori_loop(0, tiles, step, 0, unroll=8)

    for low_bit in range(3):

        @pl.when(qubit == low_bit)
        def _():
            distance = 1 << low_bit
            zero = ((sub >> low_bit) & 1) == 0

            def step(k, carry):
                at = pl.multiple_of(2 * k * TILE, TILE)
                for plane in range(2):
                    a = state[plane, pl.ds(at, TILE), :]
                    b = state[plane, pl.ds(at + TILE, TILE), :]
                    zeros = jnp.where(zero, a, pltpu.roll(b, distance, 0))
                    ones = jnp.where(zero, pltpu.roll(a, TILE - distance, 0), b)
                    sent[plane, pl.ds(pl.multiple_of(k * TILE, TILE), TILE), :] = jnp.where(value == 0, zeros, ones)
                return carry

            lax.fori_loop(0, tiles, step, 0, unroll=8)


def put_in(state, received, qubit, value):
    columns = state.shape[2]
    tiles = received.shape[1] // TILE
    sub = lax.broadcasted_iota(jnp.int32, (TILE, columns), 0)

    @pl.when(qubit >= 3)
    def _():
        def step(k, carry):
            at = pl.multiple_of(insert_bit(k, qubit - 3, value) * TILE, TILE)
            for plane in range(2):
                state[plane, pl.ds(at, TILE), :] = received[plane, pl.ds(pl.multiple_of(k * TILE, TILE), TILE), :]
            return carry

        lax.fori_loop(0, tiles, step, 0, unroll=8)

    for low_bit in range(3):

        @pl.when(qubit == low_bit)
        def _():
            distance = 1 << low_bit
            bits = (sub >> low_bit) & 1
            zero = bits == 0
            mine = bits == value

            def step(k, carry):
                at = pl.multiple_of(2 * k * TILE, TILE)
                for plane in range(2):
                    got = received[plane, pl.ds(pl.multiple_of(k * TILE, TILE), TILE), :]
                    up = pltpu.roll(got, TILE - distance, 0)
                    down = pltpu.roll(got, distance, 0)
                    a = state[plane, pl.ds(at, TILE), :]
                    b = state[plane, pl.ds(at + TILE, TILE), :]
                    first = jnp.where(zero, got, down)
                    second = jnp.where(zero, up, got)
                    state[plane, pl.ds(at, TILE), :] = jnp.where(mine, first, a)
                    state[plane, pl.ds(at + TILE, TILE), :] = jnp.where(mine, second, b)
                return carry

            lax.fori_loop(0, tiles, step, 0, unroll=8)


def shards(state, gates, control_bits, patterns, swap_qubits):
    row_count, columns = state.shape[1], state.shape[2]
    part_count = lax.axis_size("regroup")
    piece_rows = row_count // part_count
    swap_levels = lax.axis_size("swap").bit_length() - 1
    high, low = prepare(gates)
    by_permutes = part_count <= 8

    def stage(turn, current, received):
        last = turn == SWAPS

        def kernel(*refs):
            controls, pattern, qubits = refs[:3]
            high_ref, low_ref, state_in = refs[3:6]
            rest = refs[6:]
            if turn:
                got, rest = rest[0], rest[1:]
            work = rest[-1] if last and by_permutes else rest[0]
            me = lax.axis_index("swap")
            work[...] = state_in[...]
            if turn:
                slot = 1 - ((me >> ((turn - 1) % swap_levels)) & 1)
                put_in(work, got, qubits[turn - 1], slot)
            for gate in range(3 * turn, 3 * turn + 3):
                mask = (1 << controls[gate, 0]) | (1 << controls[gate, 1])
                if turn and gate == 3 * turn + 1:
                    qubit = qubits[turn - 1]
                    exchange_column_bit(work, qubit)
                    plain_gate(work, gate, high_ref, low_ref, mask & ~(1 << qubit), pattern[gate], row_count // 2)
                    exchange_column_bit(work, qubit)
                else:
                    plain_gate(work, gate, high_ref, low_ref, mask, pattern[gate], row_count // 2)
            if not last:
                slot = 1 - ((me >> (turn % swap_levels)) & 1)
                take_out(work, rest[1], qubits[turn], slot)
            elif by_permutes:
                place = lax.axis_index("regroup")
                for step in range(part_count):
                    at = pl.multiple_of((place ^ step) * piece_rows, piece_rows)
                    for plane in range(2):
                        rest[step][plane] = work[plane, pl.ds(at, piece_rows), :]

        whole = jax.ShapeDtypeStruct(state.shape, state.dtype)
        scratch = []
        if not last:
            outs = (whole, jax.ShapeDtypeStruct((2, row_count // 2, columns), state.dtype))
        elif by_permutes:
            outs = tuple(jax.ShapeDtypeStruct((2, piece_rows, columns), state.dtype) for _ in range(part_count))
            scratch = [VMEM(state.shape, state.dtype)]
        else:
            outs = (whole,)
        operands = (control_bits, patterns, swap_qubits, high, low, current) + ((received,) if turn else ())
        return pl.pallas_call(
            kernel,
            out_shape=outs,
            in_specs=in_smem(3) + in_vmem(len(operands) - 3),
            out_specs=tuple(in_vmem(len(outs))),
            scratch_shapes=scratch,
            name=f"stage{turn}",
        )(*operands)

    current, received = state, None
    for turn in range(SWAPS):
        current, sent = stage(turn, current, received)
        distance = 1 << (turn % swap_levels)
        received = lax.ppermute(sent, "swap", [(i, i ^ distance) for i in range(lax.axis_size("swap"))])
    pieces = stage(SWAPS, current, received)
    if not by_permutes:
        result = lax.all_to_all(
            pieces[0].reshape(2, part_count, piece_rows, columns), "regroup", split_axis=1, concat_axis=1, tiled=True
        )
        return result.reshape(2, row_count, columns)
    arrived = [pieces[0]]
    for step in range(1, part_count):
        arrived.append(lax.ppermute(pieces[step], "regroup", [(i, i ^ step) for i in range(part_count)]))

    def assemble(*refs):
        out, semaphores = refs[part_count:]
        place = lax.axis_index("regroup")
        copies = []
        for step in range(part_count):
            at = pl.multiple_of((place ^ step) * piece_rows, piece_rows)
            copies.append(pltpu.make_async_copy(refs[step], out.at[:, pl.ds(at, piece_rows), :], semaphores.at[step]))
        for copy in copies:
            copy.start()
        for copy in copies:
            copy.wait()

    return pl.pallas_call(
        assemble,
        out_shape=jax.ShapeDtypeStruct(state.shape, state.dtype),
        in_specs=in_vmem(part_count),
        out_specs=pl.BlockSpec(memory_space=pl.ANY),
        scratch_shapes=[pltpu.SemaphoreType.DMA((part_count,))],
        name="assemble",
    )(*arrived)


def solution(mesh):
    return jax.shard_map(
        shards,
        mesh=mesh,
        in_specs=(P(None, ("swap", "regroup"), None), P(), P(), P(), P()),
        out_specs=P(None, ("swap", "regroup"), None),
        check_vma=False,
    )
```

```python
import jax
import jax.numpy as jnp
from jax import lax
from jax.experimental import pallas as pl
from jax.experimental.pallas import tpu as pltpu
from jax.sharding import PartitionSpec as P


SWAPS = 3
TILE = 8
VMEM = pltpu.VMEM
SMEM = pltpu.SMEM


def resident(values):
    return [pltpu.with_memory_space_constraint(value, VMEM) for value in values]


def limits():
    return pltpu.CompilerParams(vmem_limit_bytes=8 << 20)


def in_vmem(count):
    return [pl.BlockSpec(memory_space=VMEM) for _ in range(count)]


def in_smem(count):
    return [pl.BlockSpec(memory_space=SMEM) for _ in range(count)]


def prepare_kernel(gates, high, low):
    order = gates.shape[-1]
    for gate in range(gates.shape[1]):
        real = gates[0, gate]
        imag = gates[1, gate]

        def put(rows, cols, value):
            top = value.astype(jnp.bfloat16)
            high[gate, rows : rows + order, cols : cols + order] = top
            low[gate, rows : rows + order, cols : cols + order] = (value - top.astype(jnp.float32)).astype(jnp.bfloat16)

        put(0, 0, real)
        put(0, order, -imag)
        put(order, 0, imag)
        put(order, order, real)


def prepare(gates):
    count, order = gates.shape[1], gates.shape[2]
    shape = VMEM((count, 2 * order, 2 * order), jnp.bfloat16)
    return pl.pallas_call(
        prepare_kernel,
        out_shape=(shape, shape),
        in_specs=in_vmem(1),
        out_specs=tuple(in_vmem(2)),
        compiler_params=limits(),
        name="prepare",
    )(*resident([gates]))


def times(left, right):
    return lax.dot_general(left, right, (((1,), (1,)), ((), ())), preferred_element_type=jnp.float32)


def plain_gate(state, gate, high, low, row_mask, pattern, chunk):
    rows_all, columns = state.shape[1], state.shape[2]
    lanes = lax.broadcasted_iota(jnp.int32, (chunk, columns), 1)
    rows = lax.broadcasted_iota(jnp.int32, (chunk, columns), 0)
    col_on = ((pattern >> (lanes // (columns // 16))) & 1) == 1
    matrix_high = high[gate]
    matrix_low = low[gate]
    for start in range(0, rows_all, chunk):
        real = state[0, start : start + chunk, :]
        imag = state[1, start : start + chunk, :]
        both = jnp.concatenate([real, imag], axis=1)
        both_high = both.astype(jnp.bfloat16)
        both_low = (both - both_high.astype(jnp.float32)).astype(jnp.bfloat16)
        new = times(both_high, matrix_high) + times(both_low, matrix_high) + times(both_high, matrix_low)
        on = (((rows + start) & row_mask) == row_mask) & col_on
        state[0, start : start + chunk, :] = jnp.where(on, new[:, :columns], real)
        state[1, start : start + chunk, :] = jnp.where(on, new[:, columns:], imag)


def insert_bit(index, bit, value):
    low = index & ((1 << bit) - 1)
    return ((index >> bit) << (bit + 1)) | low | (value << bit)


def tile_at(ref, plane, index):
    return ref[plane, pl.ds(pl.multiple_of(index * TILE, TILE), TILE), :]


def in_groups(count, move):
    group = min(count, 16)

    def step(turn, carry):
        stores = []
        for inner in range(group):
            stores += move(turn * group + inner)
        for ref, plane, index, value in stores:
            ref[plane, pl.ds(pl.multiple_of(index * TILE, TILE), TILE), :] = value
        return carry

    lax.fori_loop(0, count // group, step, 0)


def row_bits(columns):
    return lax.broadcasted_iota(jnp.int32, (TILE, columns), 0)


def exchange_column_bit(state, qubit):
    rows_all, columns = state.shape[1], state.shape[2]
    half = columns // 2
    lane_low = lax.broadcasted_iota(jnp.int32, (TILE, columns), 1) < half
    sub = row_bits(columns)
    tiles = rows_all // TILE

    @pl.when(qubit >= 3)
    def _():
        def move(k):
            first = insert_bit(k, qubit - 3, 0)
            second = insert_bit(k, qubit - 3, 1)
            stores = []
            for plane in range(2):
                a = tile_at(state, plane, first)
                b = tile_at(state, plane, second)
                stores.append((state, plane, first, jnp.where(lane_low, a, pltpu.roll(b, half, 1))))
                stores.append((state, plane, second, jnp.where(lane_low, pltpu.roll(a, half, 1), b)))
            return stores

        in_groups(tiles // 2, move)

    for low_bit in range(3):

        @pl.when(qubit == low_bit)
        def _():
            distance = 1 << low_bit
            zero = ((sub >> low_bit) & 1) == 0
            keep = zero == lane_low

            def move(k):
                stores = []
                for plane in range(2):
                    a = tile_at(state, plane, k)
                    turned = pltpu.roll(a, half, 1)
                    partner = jnp.where(zero, pltpu.roll(turned, TILE - distance, 0), pltpu.roll(turned, distance, 0))
                    stores.append((state, plane, k, jnp.where(keep, a, partner)))
                return stores

            in_groups(tiles, move)


def take_out(state, sent, qubit, value):
    tiles = sent.shape[1] // TILE
    sub = row_bits(state.shape[2])

    @pl.when(qubit >= 3)
    def _():
        def move(k):
            at = insert_bit(k, qubit - 3, value)
            return [(sent, plane, k, tile_at(state, plane, at)) for plane in range(2)]

        in_groups(tiles, move)

    for low_bit in range(3):

        @pl.when(qubit == low_bit)
        def _():
            distance = 1 << low_bit
            zero = ((sub >> low_bit) & 1) == 0

            def move(k):
                stores = []
                for plane in range(2):
                    a = tile_at(state, plane, 2 * k)
                    b = tile_at(state, plane, 2 * k + 1)
                    zeros = jnp.where(zero, a, pltpu.roll(b, distance, 0))
                    ones = jnp.where(zero, pltpu.roll(a, TILE - distance, 0), b)
                    stores.append((sent, plane, k, jnp.where(value == 0, zeros, ones)))
                return stores

            in_groups(tiles, move)


def put_in(state, received, qubit, value):
    tiles = received.shape[1] // TILE
    sub = row_bits(state.shape[2])

    @pl.when(qubit >= 3)
    def _():
        def move(k):
            at = insert_bit(k, qubit - 3, value)
            return [(state, plane, at, tile_at(received, plane, k)) for plane in range(2)]

        in_groups(tiles, move)

    for low_bit in range(3):

        @pl.when(qubit == low_bit)
        def _():
            distance = 1 << low_bit
            bits = (sub >> low_bit) & 1
            zero = bits == 0
            mine = bits == value

            def move(k):
                stores = []
                for plane in range(2):
                    got = tile_at(received, plane, k)
                    a = tile_at(state, plane, 2 * k)
                    b = tile_at(state, plane, 2 * k + 1)
                    first = jnp.where(zero, got, pltpu.roll(got, distance, 0))
                    second = jnp.where(zero, pltpu.roll(got, TILE - distance, 0), got)
                    stores.append((state, plane, 2 * k, jnp.where(mine, first, a)))
                    stores.append((state, plane, 2 * k + 1, jnp.where(mine, second, b)))
                return stores

            in_groups(tiles, move)


def shards(state, gates, control_bits, patterns, swap_qubits):
    row_count, columns = state.shape[1], state.shape[2]
    part_count = lax.axis_size("regroup")
    piece_rows = row_count // part_count
    swap_levels = lax.axis_size("swap").bit_length() - 1
    high, low = prepare(gates)
    by_permutes = part_count <= 8

    def stage(turn, current, received):
        last = turn == SWAPS

        def kernel(*refs):
            controls, pattern, qubits = refs[:3]
            high_ref, low_ref, state_in = refs[3:6]
            rest = refs[6:]
            if turn:
                got, rest = rest[0], rest[1:]
            work = rest[-1] if last and by_permutes else rest[0]
            me = lax.axis_index("swap")
            work[...] = state_in[...]
            if turn:
                slot = 1 - ((me >> ((turn - 1) % swap_levels)) & 1)
                put_in(work, got, qubits[turn - 1], slot)
            for gate in range(3 * turn, 3 * turn + 3):
                mask = (1 << controls[0, gate]) | (1 << controls[1, gate])
                if turn and gate == 3 * turn + 1:
                    qubit = qubits[turn - 1]
                    exchange_column_bit(work, qubit)
                    plain_gate(work, gate, high_ref, low_ref, mask & ~(1 << qubit), pattern[gate], row_count // 2)
                    exchange_column_bit(work, qubit)
                else:
                    plain_gate(work, gate, high_ref, low_ref, mask, pattern[gate], row_count // 2)
            if not last:
                slot = 1 - ((me >> (turn % swap_levels)) & 1)
                take_out(work, rest[1], qubits[turn], slot)
            elif by_permutes:
                place = lax.axis_index("regroup")
                for step in range(part_count):
                    at = pl.multiple_of((place ^ step) * piece_rows, piece_rows)
                    for plane in range(2):
                        rest[step][plane] = work[plane, pl.ds(at, piece_rows), :]

        whole = VMEM(state.shape, state.dtype)
        scratch = []
        if not last:
            outs = (whole, VMEM((2, row_count // 2, columns), state.dtype))
        elif by_permutes:
            outs = tuple(VMEM((2, piece_rows, columns), state.dtype) for _ in range(part_count))
            scratch = [VMEM(state.shape, state.dtype)]
        else:
            outs = (whole,)
        operands = [control_bits.T, patterns, swap_qubits]
        operands += resident([high, low, current] + ([received] if turn else []))
        return pl.pallas_call(
            kernel,
            out_shape=outs,
            in_specs=in_smem(3) + in_vmem(len(operands) - 3),
            out_specs=tuple(in_vmem(len(outs))),
            scratch_shapes=scratch,
            compiler_params=limits(),
            name=f"stage{turn}",
        )(*operands)

    current, received = state, None
    for turn in range(SWAPS):
        current, sent = stage(turn, current, received)
        distance = 1 << (turn % swap_levels)
        received = lax.ppermute(sent, "swap", [(i, i ^ distance) for i in range(lax.axis_size("swap"))])
    pieces = stage(SWAPS, current, received)
    if not by_permutes:
        result = lax.all_to_all(
            pieces[0].reshape(2, part_count, piece_rows, columns), "regroup", split_axis=1, concat_axis=1, tiled=True
        )
        return result.reshape(2, row_count, columns)
    arrived = {0: pieces[0]}
    for step in list(range(part_count // 2, part_count)) + list(range(1, part_count // 2)):
        arrived[step] = lax.ppermute(pieces[step], "regroup", [(i, i ^ step) for i in range(part_count)])
    arrived = [arrived[step] for step in range(part_count)]

    def assemble(*refs):
        out, semaphores = refs[part_count:]
        place = lax.axis_index("regroup")
        copies = []
        for step in range(part_count):
            at = pl.multiple_of((place ^ step) * piece_rows, piece_rows)
            copies.append(pltpu.make_async_copy(refs[step], out.at[:, pl.ds(at, piece_rows), :], semaphores.at[step]))
        for copy in copies:
            copy.start()
        for copy in copies:
            copy.wait()

    return pl.pallas_call(
        assemble,
        out_shape=jax.ShapeDtypeStruct(state.shape, state.dtype),
        in_specs=in_vmem(part_count),
        out_specs=pl.BlockSpec(memory_space=pl.ANY),
        scratch_shapes=[pltpu.SemaphoreType.DMA((part_count,))],
        compiler_params=limits(),
        name="assemble",
    )(*resident(arrived))


def solution(mesh):
    return jax.shard_map(
        shards,
        mesh=mesh,
        in_specs=(P(None, ("swap", "regroup"), None), P(), P(), P(), P()),
        out_specs=P(None, ("swap", "regroup"), None),
        check_vma=False,
    )
```

```python
import jax
import jax.numpy as jnp
from jax import lax
from jax.experimental import pallas as pl
from jax.experimental.pallas import tpu as pltpu
from jax.sharding import PartitionSpec as P


SWAPS = 3
TILE = 8
VMEM = pltpu.VMEM
SMEM = pltpu.SMEM


def resident(values):
    return [pltpu.with_memory_space_constraint(value, VMEM) for value in values]


def limits():
    return pltpu.CompilerParams(vmem_limit_bytes=8 << 20)


def in_vmem(count):
    return [pl.BlockSpec(memory_space=VMEM) for _ in range(count)]


def in_smem(count):
    return [pl.BlockSpec(memory_space=SMEM) for _ in range(count)]


def prepare_kernel(gates, high, low):
    order = gates.shape[-1]
    for gate in range(gates.shape[1]):
        real = gates[0, gate]
        imag = gates[1, gate]

        def put(rows, cols, value):
            top = value.astype(jnp.bfloat16)
            high[gate, rows : rows + order, cols : cols + order] = top
            low[gate, rows : rows + order, cols : cols + order] = (value - top.astype(jnp.float32)).astype(jnp.bfloat16)

        put(0, 0, real)
        put(0, order, -imag)
        put(order, 0, imag)
        put(order, order, real)


def prepare(gates):
    count, order = gates.shape[1], gates.shape[2]
    shape = VMEM((count, 2 * order, 2 * order), jnp.bfloat16)
    return pl.pallas_call(
        prepare_kernel,
        out_shape=(shape, shape),
        in_specs=in_vmem(1),
        out_specs=tuple(in_vmem(2)),
        compiler_params=limits(),
        name="prepare",
    )(*resident([gates]))


def times(left, right):
    return lax.dot_general(left, right, (((1,), (1,)), ((), ())), preferred_element_type=jnp.float32)


def column_on(pattern, rows, columns):
    groups = lax.broadcasted_iota(jnp.int32, (rows, columns), 1) // (columns // 16)
    return ((pattern >> groups) & 1) == 1


def gated(both, gate, high, low, on):
    both_high = both.astype(jnp.bfloat16)
    both_low = (both - both_high.astype(jnp.float32)).astype(jnp.bfloat16)
    new = times(both_high, high[gate]) + times(both_low, high[gate]) + times(both_high, low[gate])
    return jnp.where(jnp.concatenate([on, on], axis=1), new, both)


def plain_gate(state, gate, weights, row_mask, pattern, row_base, chunk):
    rows_all, columns = state.shape[1], state.shape[2]
    rows = lax.broadcasted_iota(jnp.int32, (chunk, columns), 0) + row_base
    col_on = column_on(pattern, chunk, columns)
    for start in range(0, rows_all, chunk):
        both = jnp.concatenate([state[plane, start : start + chunk, :] for plane in range(2)], axis=1)
        on = (((rows + start) & row_mask) == row_mask) & col_on
        both = gated(both, gate, *weights, on)
        for plane in range(2):
            state[plane, start : start + chunk, :] = both[:, plane * columns : (plane + 1) * columns]


def pair_gate(state, gate, weights, row_mask, pattern, row_base, ranges, count):
    columns = state.shape[2]
    half = columns // 2
    iota = lax.broadcasted_iota(jnp.int32, (count, columns), 0) + row_base
    lane_low = lax.broadcasted_iota(jnp.int32, (count, columns), 1) < half
    col_on = column_on(pattern, count, columns)
    lowers, uppers, masks = [], [], []
    for first, second in ranges:
        lower = [state[plane, first : first + count, :] for plane in range(2)]
        upper = [state[plane, second : second + count, :] for plane in range(2)]
        lowers.append([jnp.where(lane_low, a, pltpu.roll(b, half, 1)) for a, b in zip(lower, upper)])
        uppers.append([jnp.where(lane_low, pltpu.roll(a, half, 1), b) for a, b in zip(lower, upper)])
        masks.append((((iota + first) & row_mask) == row_mask) & col_on)
    both = jnp.concatenate([jnp.concatenate(part, axis=1) for part in lowers + uppers], axis=0)
    both = gated(both, gate, *weights, jnp.concatenate(masks + masks, axis=0))
    for index, (first, second) in enumerate(ranges):
        left = both[index * count : (index + 1) * count]
        right = both[(index + len(ranges)) * count : (index + len(ranges) + 1) * count]
        for plane in range(2):
            a = left[:, plane * columns : (plane + 1) * columns]
            b = right[:, plane * columns : (plane + 1) * columns]
            state[plane, first : first + count, :] = jnp.where(lane_low, a, pltpu.roll(b, half, 1))
            state[plane, second : second + count, :] = jnp.where(lane_low, pltpu.roll(a, half, 1), b)


def insert_bit(index, bit, value):
    low = index & ((1 << bit) - 1)
    return ((index >> bit) << (bit + 1)) | low | (value << bit)


def tile_at(ref, plane, index):
    return ref[plane, pl.ds(pl.multiple_of(index * TILE, TILE), TILE), :]


def in_groups(count, move):
    group = min(count, 16)

    def step(turn, carry):
        stores = []
        for inner in range(group):
            stores += move(turn * group + inner)
        for ref, plane, index, value in stores:
            ref[plane, pl.ds(pl.multiple_of(index * TILE, TILE), TILE), :] = value
        return carry

    lax.fori_loop(0, count // group, step, 0)


def permute_order(count):
    half = count // 2
    far = list(range(half, count))
    near = list(range(1, half))
    order = far[:2]
    for left, right in zip(near[1:] + near[:1], far[2:] + near[:1]):
        order += [left, right] if right in far else [left]
    return order


def row_bits(columns):
    return lax.broadcasted_iota(jnp.int32, (TILE, columns), 0)


def exchange_column_bit(state, qubit):
    rows_all, columns = state.shape[1], state.shape[2]
    half = columns // 2
    lane_low = lax.broadcasted_iota(jnp.int32, (TILE, columns), 1) < half
    sub = row_bits(columns)
    tiles = rows_all // TILE

    @pl.when(qubit >= 3)
    def _():
        def move(k):
            first = insert_bit(k, qubit - 3, 0)
            second = insert_bit(k, qubit - 3, 1)
            stores = []
            for plane in range(2):
                a = tile_at(state, plane, first)
                b = tile_at(state, plane, second)
                stores.append((state, plane, first, jnp.where(lane_low, a, pltpu.roll(b, half, 1))))
                stores.append((state, plane, second, jnp.where(lane_low, pltpu.roll(a, half, 1), b)))
            return stores

        in_groups(tiles // 2, move)

    for low_bit in range(3):

        @pl.when(qubit == low_bit)
        def _():
            distance = 1 << low_bit
            zero = ((sub >> low_bit) & 1) == 0
            keep = zero == lane_low

            def move(k):
                stores = []
                for plane in range(2):
                    a = tile_at(state, plane, k)
                    turned = pltpu.roll(a, half, 1)
                    partner = jnp.where(zero, pltpu.roll(turned, TILE - distance, 0), pltpu.roll(turned, distance, 0))
                    stores.append((state, plane, k, jnp.where(keep, a, partner)))
                return stores

            in_groups(tiles, move)


def take_out(state, sent, qubit, value):
    tiles = sent.shape[1] // TILE
    sub = row_bits(state.shape[2])

    @pl.when(qubit >= 3)
    def _():
        def move(k):
            at = insert_bit(k, qubit - 3, value)
            return [(sent, plane, k, tile_at(state, plane, at)) for plane in range(2)]

        in_groups(tiles, move)

    for low_bit in range(3):

        @pl.when(qubit == low_bit)
        def _():
            distance = 1 << low_bit
            zero = ((sub >> low_bit) & 1) == 0

            def move(k):
                stores = []
                for plane in range(2):
                    a = tile_at(state, plane, 2 * k)
                    b = tile_at(state, plane, 2 * k + 1)
                    zeros = jnp.where(zero, a, pltpu.roll(b, distance, 0))
                    ones = jnp.where(zero, pltpu.roll(a, TILE - distance, 0), b)
                    stores.append((sent, plane, k, jnp.where(value == 0, zeros, ones)))
                return stores

            in_groups(tiles, move)


def put_in(state, received, qubit, value):
    tiles = received.shape[1] // TILE
    sub = row_bits(state.shape[2])

    @pl.when(qubit >= 3)
    def _():
        def move(k):
            at = insert_bit(k, qubit - 3, value)
            return [(state, plane, at, tile_at(received, plane, k)) for plane in range(2)]

        in_groups(tiles, move)

    for low_bit in range(3):

        @pl.when(qubit == low_bit)
        def _():
            distance = 1 << low_bit
            bits = (sub >> low_bit) & 1
            zero = bits == 0
            mine = bits == value

            def move(k):
                stores = []
                for plane in range(2):
                    got = tile_at(received, plane, k)
                    a = tile_at(state, plane, 2 * k)
                    b = tile_at(state, plane, 2 * k + 1)
                    first = jnp.where(zero, got, pltpu.roll(got, distance, 0))
                    second = jnp.where(zero, pltpu.roll(got, TILE - distance, 0), got)
                    stores.append((state, plane, 2 * k, jnp.where(mine, first, a)))
                    stores.append((state, plane, 2 * k + 1, jnp.where(mine, second, b)))
                return stores

            in_groups(tiles, move)


def swap_row_bits(source, state, low, high):
    sub = row_bits(state.shape[2])
    tiles = state.shape[1] // TILE
    for low_bit in range(3):

        @pl.when(low == low_bit)
        def _():
            distance = 1 << low_bit
            zero = ((sub >> low_bit) & 1) == 0

            def move(k):
                at_zero = insert_bit(k, high - 3, 0)
                at_one = insert_bit(k, high - 3, 1)
                stores = []
                for plane in range(2):
                    a = tile_at(source, plane, at_zero)
                    b = tile_at(source, plane, at_one)
                    stores.append((state, plane, at_zero, jnp.where(zero, a, pltpu.roll(b, distance, 0))))
                    stores.append((state, plane, at_one, jnp.where(zero, pltpu.roll(a, TILE - distance, 0), b)))
                return stores

            in_groups(tiles // 2, move)


class Plan:
    def __init__(self, qubits, row_count):
        self.q = [qubits[turn] for turn in range(SWAPS)]
        q0, q1, q2 = self.q
        self.bits = row_count.bit_length() - 1
        top = self.bits - 1
        self.apart = (q0 != q1) & (q0 != q2) & (q1 != q2)
        route = jnp.where(self.apart, q2, q0)
        cross = jnp.where(q1 != q0, q1, jnp.where(q0 == top, top - 1, top))
        spare = jnp.int32(top)
        for _ in range(2):
            spare = spare - ((spare == route) | (spare == cross)).astype(jnp.int32)
        target = jnp.where(self.apart, q0, spare)
        self.special = [target, route, cross]
        self.at = []
        free = jnp.int32(2)
        for bit in self.special:
            free = free + 1
            for _ in range(3):
                free = free + ((free == route) | (free == cross) | (free == target)).astype(jnp.int32)
            self.at.append(jnp.where(bit >= 3, bit, free))
        self.any_low = (route < 3) | (cross < 3) | (target < 3)
        self.target_bit, self.route_bit, self.cross_bit = self.bits - 3, self.bits - 2, self.bits - 1

    def place(self, bit):
        place = bit
        for special, at in zip(self.special, self.at):
            place = jnp.where(place == special, at, jnp.where(place == at, special, place))
        below = sum((place > at).astype(jnp.int32) for at in self.at)
        return 1 << jnp.where(bit == self.special[0], self.target_bit, place - below)

    def tile(self, rest, target, route, cross):
        a, b, c = (at - 3 for at in self.at)
        low = jnp.minimum(jnp.minimum(a, b), c)
        high = jnp.maximum(jnp.maximum(a, b), c)
        tile = insert_bit(insert_bit(insert_bit(rest, low, 0), a + b + c - low - high, 0), high, 0)
        return tile | (target << a) | (route << b) | (cross << c)

    def mask(self, gate, controls, me):
        q0, q1, q2 = self.q
        stage = gate // 3
        never = jnp.int32(1 << 20)
        from_core = jnp.where((me & 1) == 1, 0, never)
        from_chip = jnp.where(((me >> 1) & 1) == 1, 0, never)
        total = jnp.int32(0)
        for which in range(2):
            c = controls[which, gate]
            bit = self.place(c)
            if stage == 3:
                bit = jnp.where(self.apart & (c == q2), 1 << self.target_bit, bit)
            else:
                bit = jnp.where(self.apart & (c == q2), from_core, bit)
            bit = jnp.where(c == q1, (1 << self.cross_bit) if stage >= 2 else from_chip, bit)
            if stage:
                bit = jnp.where(c == q0, 1 << self.route_bit, bit)
                if gate % 3 == 1:
                    bit = jnp.where(c == self.q[stage - 1], 0, bit)
            else:
                bit = jnp.where(c == q0, jnp.where(self.apart, 1 << self.target_bit, from_core), bit)
            total = total | bit
        return total


def shards(state, gates, control_bits, patterns, swap_qubits):
    row_count, columns = state.shape[1], state.shape[2]
    part_count = lax.axis_size("regroup")
    swap_count = lax.axis_size("swap")
    piece_rows = row_count // part_count
    swap_levels = swap_count.bit_length() - 1
    by_permutes = part_count <= 8
    controls = control_bits.T
    half_rows, quarter_rows = row_count // 2, row_count // 4

    def array(rows):
        return VMEM((2, rows, columns), state.dtype)

    def call(kernel, name, scalars, values, outs, scratch=(), last_in_place=False):
        outs = tuple(outs)
        specs = in_vmem(len(values))
        values = list(values)
        if last_in_place:
            specs[-1] = pl.BlockSpec(memory_space=pl.ANY)
            values = resident(values[:-1]) + values[-1:]
        else:
            values = resident(values)
        return pl.pallas_call(
            kernel,
            out_shape=outs,
            in_specs=in_smem(len(scalars)) + specs,
            out_specs=tuple((in_smem if out.dtype == jnp.int32 else in_vmem)(1)[0] for out in outs),
            scratch_shapes=list(scratch),
            compiler_params=limits(),
            name=name,
        )(*scalars, *values)

    scalars = (controls, patterns, swap_qubits)

    def give_pieces(work, pieces):
        place = lax.axis_index("regroup")
        for step in range(part_count):
            at = pl.multiple_of((place ^ step) * piece_rows, piece_rows)
            for plane in range(2):
                pieces[step][plane] = work[plane, pl.ds(at, piece_rows), :]

    def regroup(pieces):
        if not by_permutes:
            whole = pieces[0].reshape(2, part_count, piece_rows, columns)
            result = lax.all_to_all(whole, "regroup", split_axis=1, concat_axis=1, tiled=True)
            return result.reshape(2, row_count, columns)
        arrived = {0: pieces[0]}
        for step in permute_order(part_count):
            arrived[step] = lax.ppermute(pieces[step], "regroup", [(i, i ^ step) for i in range(part_count)])
        order = list(arrived)

        def assemble(*refs):
            out, semaphores = refs[part_count:]
            place = lax.axis_index("regroup")
            copies = []
            for index, step in enumerate(order):
                at = pl.multiple_of((place ^ step) * piece_rows, piece_rows)
                copies.append(pltpu.make_async_copy(refs[index], out.at[:, pl.ds(at, piece_rows), :], semaphores.at[index]))
            for copy in copies:
                copy.start()
            for copy in copies:
                copy.wait()

        return pl.pallas_call(
            assemble,
            out_shape=pltpu.HBM(state.shape, state.dtype),
            in_specs=in_vmem(part_count),
            out_specs=pl.BlockSpec(memory_space=pltpu.HBM),
            scratch_shapes=[pltpu.SemaphoreType.DMA((part_count,))],
            compiler_params=limits(),
            name="assemble",
        )(*resident(arrived[step] for step in order))

    def stage(turn, weights, current, received):
        last = turn == SWAPS

        def kernel(*refs):
            controls, pattern, qubits = refs[:3]
            high_ref, low_ref, state_in = refs[3:6]
            rest = refs[6:]
            if turn:
                got, rest = rest[0], rest[1:]
            work = rest[-1] if last and by_permutes else rest[0]
            me = lax.axis_index("swap")
            if turn:
                work[...] = state_in[...]
            else:
                pltpu.sync_copy(state_in, work)
            if turn:
                slot = 1 - ((me >> ((turn - 1) % swap_levels)) & 1)
                put_in(work, got, qubits[turn - 1], slot)
            for gate in range(3 * turn, 3 * turn + 3):
                mask = (1 << controls[0, gate]) | (1 << controls[1, gate])
                pair = turn and gate == 3 * turn + 1
                if pair:
                    qubit = qubits[turn - 1]
                    mask = mask & ~(1 << qubit)
                    exchange_column_bit(work, qubit)
                plain_gate(work, gate, (high_ref, low_ref), mask, pattern[gate], 0, half_rows)
                if pair:
                    exchange_column_bit(work, qubit)
            if not last:
                slot = 1 - ((me >> (turn % swap_levels)) & 1)
                take_out(work, rest[1], qubits[turn], slot)
            elif by_permutes:
                give_pieces(work, rest[:part_count])

        scratch = []
        if not last:
            outs = (array(row_count), array(half_rows))
        elif by_permutes:
            outs = (array(piece_rows),) * part_count
            scratch = [array(row_count)]
        else:
            outs = (array(row_count),)
        values = [*weights, current] + ([received] if turn else [])
        return call(kernel, f"stage{turn}", scalars, values, outs, scratch, last_in_place=not turn)

    def one_by_one(weights):
        current, received = state, None
        for turn in range(SWAPS):
            current, sent = stage(turn, weights, current, received)
            received = from_partner(sent, 1 << (turn % swap_levels))
        return regroup(stage(SWAPS, weights, current, received))

    def from_partner(sent, distance):
        return lax.ppermute(sent, "swap", [(i, i ^ distance) for i in range(swap_count)])

    if not (by_permutes and swap_levels == 2):
        return one_by_one(prepare(gates))

    quarter_tiles = quarter_rows // TILE

    def pack(*refs):
        qubits, state_in = refs[:2]
        messages, case, work = refs[2:6], refs[6], refs[7]
        plan = Plan(qubits, row_count)
        case[0] = jnp.where(qubits[0] == qubits[1], 2, jnp.where(plan.apart, 0, 1))
        me = lax.axis_index("swap")

        def send(source):
            for distance in (2, 3, 1, 0):
                to = me ^ distance

                def move(k):
                    at = plan.tile(k & (quarter_tiles // 2 - 1), k // (quarter_tiles // 2), to & 1, to >> 1)
                    return [(messages[distance], plane, k, tile_at(source, plane, at)) for plane in range(2)]

                in_groups(quarter_tiles, move)

        @pl.when(plan.any_low)
        def _():
            work[...] = state_in[...]
            for low, high in zip(plan.special, plan.at):
                swap_row_bits(work, work, low, high)
            send(work)

        @pl.when(jnp.logical_not(plan.any_low))
        def _():
            send(state_in)

    outs = (array(quarter_rows),) * 4 + (jax.ShapeDtypeStruct((1,), jnp.int32),)
    *messages, case = call(pack, "pack", (swap_qubits,), (state,), outs, [array(row_count)])
    arrived = {0: messages[0]}
    for distance in (2, 3, 1):
        with jax.named_scope(f"from{distance}"):
            arrived[distance] = from_partner(messages[distance], distance)
    with jax.named_scope("weights"):
        weights = prepare(gates)

    def run_gates(work, plan, refs, numbers, row_base, apart=None):
        controls, pattern, weights = refs
        me = lax.axis_index("swap")
        halves = range(0, work.shape[1], half_rows)
        for gate in numbers:
            args = (gate, weights, plan.mask(gate, controls, me), pattern[gate])
            if gate == 4:
                for start in halves:
                    pair_gate(work, *args, row_base, [(start, start + quarter_rows)], quarter_rows)
            elif gate == 7:
                for start in range(0, half_rows, quarter_rows):
                    pair_gate(work, *args, row_base, [(start, start + half_rows)], quarter_rows)
            elif gate == 10 and apart:
                eighth = quarter_rows // 2
                for start in halves:
                    ranges = [(at, at + eighth) for at in (start, start + quarter_rows)]
                    pair_gate(work, *args, row_base, ranges, eighth)
            elif gate == 10:
                qubit = jnp.where(plan.q[2] == plan.q[0], plan.route_bit, plan.cross_bit)
                exchange_column_bit(work, qubit)
                plain_gate(work, *args, row_base, half_rows)
                exchange_column_bit(work, qubit)
            else:
                plain_gate(work, *args, row_base, half_rows)

    def unpack(work, spare, plan, apart, pieces):
        def move(k):
            rest = k & (quarter_tiles // 2 - 1)
            target, route, cross = ((k // (quarter_tiles // 2 << up)) & 1 for up in range(3))
            at = plan.tile(rest, route, target, cross) if apart else plan.tile(rest, target, route, cross)
            return [(spare, plane, at, tile_at(work, plane, k)) for plane in range(2)]

        in_groups(row_count // TILE, move)
        for low, high in zip(plan.special, plan.at):
            swap_row_bits(spare, spare, low, high)
        give_pieces(spare, pieces)

    def place_quarter(half, source, value):
        at = pl.multiple_of((source & 1) * quarter_rows, quarter_rows)
        half[:, pl.ds(at, quarter_rows), :] = value[...]

    def near(*refs):
        controls, pattern, qubits, high_ref, low_ref, own, core, work = refs
        me = lax.axis_index("swap")
        place_quarter(work, me, own)
        place_quarter(work, me ^ 1, core)
        plan = Plan(qubits, row_count)
        run_gates(work, plan, (controls, pattern, (high_ref, low_ref)), range(7), (me >> 1) * half_rows)

    values = [*weights, arrived[0], arrived[1]]
    with jax.named_scope("near"):
        near_rows = call(near, "near", scalars, values, (array(half_rows),))[0]

    def merged(numbers, apart, finish):
        def kernel(*refs):
            controls, pattern, qubits, high_ref, low_ref, near_ref, third, fourth = refs[:8]
            far, work = refs[-2:]
            plan = Plan(qubits, row_count)
            me = lax.axis_index("swap")
            gate_refs = (controls, pattern, (high_ref, low_ref))
            place_quarter(far, me ^ 2, third)
            place_quarter(far, me ^ 3, fourth)
            here = pl.multiple_of((me >> 1) * half_rows, half_rows)
            there = pl.multiple_of(half_rows - here, half_rows)
            run_gates(far, plan, gate_refs, range(7), there)
            work[:, pl.ds(here, half_rows), :] = near_ref[...]
            work[:, pl.ds(there, half_rows), :] = far[...]
            run_gates(work, plan, gate_refs, numbers, 0, apart)
            finish(work, plan, refs[8:-2])

        return kernel, [*weights, near_rows, arrived[2], arrived[3]], [array(half_rows), array(row_count)]

    def all_apart():
        def finish(work, plan, refs):
            unpack(work, refs[-1], plan, True, refs[:part_count])

        kernel, values, scratch = merged(range(7, 12), True, finish)
        outs = (array(piece_rows),) * part_count
        return regroup(call(kernel, "merged", scalars, values, outs, [array(row_count)] + scratch))

    def core_again():
        def slot_and_bit(plan):
            return 1 - (lax.axis_index("swap") & 1), jnp.where(plan.q[2] == plan.q[0], plan.route_bit, plan.cross_bit)

        def finish(work, plan, refs):
            refs[0][...] = work[...]
            slot, bit = slot_and_bit(plan)
            take_out(work, refs[1], bit, slot)

        kernel, values, scratch = merged(range(7, 9), False, finish)
        current, sent = call(kernel, "merged_send", scalars, values, (array(row_count), array(half_rows)), scratch)
        received = from_partner(sent, 1)

        def last(*refs):
            controls, pattern, qubits, high_ref, low_ref, current_ref, got = refs[:7]
            work, spare = refs[-2:]
            plan = Plan(qubits, row_count)
            slot, bit = slot_and_bit(plan)
            work[...] = current_ref[...]
            put_in(work, got, bit, slot)
            run_gates(work, plan, (controls, pattern, (high_ref, low_ref)), range(9, 12), 0, False)
            unpack(work, spare, plan, False, refs[7:-2])

        outs = (array(piece_rows),) * part_count
        values = [*weights, current, received]
        return regroup(call(last, "last", scalars, values, outs, [array(row_count)] * 2))

    return lax.switch(case[0], [all_apart, core_again, lambda: one_by_one(weights)])


def solution(mesh):
    return jax.shard_map(
        shards,
        mesh=mesh,
        in_specs=(P(None, ("swap", "regroup"), None), P(), P(), P(), P()),
        out_specs=P(None, ("swap", "regroup"), None),
        check_vma=False,
    )
```

```python
import jax
import jax.numpy as jnp
from jax import lax
from jax.experimental import pallas as pl
from jax.experimental.pallas import tpu as pltpu
from jax.sharding import PartitionSpec as P


SWAPS = 3
TILE = 8
VMEM = pltpu.VMEM
SMEM = pltpu.SMEM


def resident(values):
    return [pltpu.with_memory_space_constraint(value, VMEM) for value in values]


def held_scalars(values):
    return [pltpu.with_memory_space_constraint(value, SMEM) for value in values]


def limits():
    return pltpu.CompilerParams(vmem_limit_bytes=8 << 20)


def in_vmem(count):
    return [pl.BlockSpec(memory_space=VMEM) for _ in range(count)]


def in_smem(count):
    return [pl.BlockSpec(memory_space=SMEM) for _ in range(count)]


def prepare(gates, scalars, outs, fill):
    count, order = gates.shape[1], gates.shape[2]
    shape = VMEM((count, 2 * order, 2 * order), jnp.bfloat16)

    def kernel(*refs):
        source = refs[len(scalars)]
        high, low = refs[len(scalars) + 1 : len(scalars) + 3]
        held, semaphores = refs[-2:]
        copies = [pltpu.make_async_copy(source.at[:, gate], held.at[:, gate], semaphores.at[gate]) for gate in range(count)]
        for copy in copies:
            copy.start()
        fill(refs[: len(scalars)], refs[len(scalars) + 3 : -2])
        for gate in range(count):
            copies[gate].wait()
            real, imag = held[0, gate], held[1, gate]
            for row, col, value in ((0, 0, real), (0, 1, -imag), (1, 0, imag), (1, 1, real)):
                top = value.astype(jnp.bfloat16)
                at = (gate, slice(row * order, row * order + order), slice(col * order, col * order + order))
                high[at] = top
                low[at] = (value - top.astype(jnp.float32)).astype(jnp.bfloat16)

    high, low, *rest = pl.pallas_call(
        kernel,
        out_shape=(shape, shape, *outs),
        in_specs=in_smem(len(scalars)) + [pl.BlockSpec(memory_space=pltpu.HBM)],
        out_specs=(*in_vmem(2), *in_smem(len(outs))),
        scratch_shapes=[VMEM(gates.shape, gates.dtype), pltpu.SemaphoreType.DMA((count,))],
        compiler_params=limits(),
        name="prepare",
    )(*held_scalars(scalars), pltpu.with_memory_space_constraint(gates, pltpu.HBM))
    return (high, low), rest


def times(left, right):
    return lax.dot_general(left, right, (((1,), (1,)), ((), ())), preferred_element_type=jnp.float32)


def column_on(pattern, rows, columns):
    groups = lax.broadcasted_iota(jnp.int32, (rows, columns), 1) // (columns // 16)
    return ((pattern >> groups) & 1) == 1


def gated(both, gate, high, low, on):
    both_high = both.astype(jnp.bfloat16)
    both_low = (both - both_high.astype(jnp.float32)).astype(jnp.bfloat16)
    new = times(both_high, high[gate]) + times(both_low, high[gate]) + times(both_high, low[gate])
    return jnp.where(jnp.concatenate([on, on], axis=1), new, both)


def plain_gate(state, gate, weights, row_mask, pattern, row_base, chunk):
    rows_all, columns = state.shape[1], state.shape[2]
    rows = lax.broadcasted_iota(jnp.int32, (chunk, columns), 0) + row_base
    col_on = column_on(pattern, chunk, columns)
    for start in range(0, rows_all, chunk):
        both = jnp.concatenate([state[plane, start : start + chunk, :] for plane in range(2)], axis=1)
        on = (((rows + start) & row_mask) == row_mask) & col_on
        both = gated(both, gate, *weights, on)
        for plane in range(2):
            state[plane, start : start + chunk, :] = both[:, plane * columns : (plane + 1) * columns]


def pair_gate(state, gate, weights, row_mask, pattern, row_base, ranges, count):
    columns = state.shape[2]
    half = columns // 2
    iota = lax.broadcasted_iota(jnp.int32, (count, columns), 0) + row_base
    lane_low = lax.broadcasted_iota(jnp.int32, (count, columns), 1) < half
    col_on = column_on(pattern, count, columns)
    lowers, uppers, masks = [], [], []
    for first, second in ranges:
        lower = [state[plane, first : first + count, :] for plane in range(2)]
        upper = [state[plane, second : second + count, :] for plane in range(2)]
        lowers.append([jnp.where(lane_low, a, pltpu.roll(b, half, 1)) for a, b in zip(lower, upper)])
        uppers.append([jnp.where(lane_low, pltpu.roll(a, half, 1), b) for a, b in zip(lower, upper)])
        masks.append((((iota + first) & row_mask) == row_mask) & col_on)
    both = jnp.concatenate([jnp.concatenate(part, axis=1) for part in lowers + uppers], axis=0)
    both = gated(both, gate, *weights, jnp.concatenate(masks + masks, axis=0))
    for index, (first, second) in enumerate(ranges):
        left = both[index * count : (index + 1) * count]
        right = both[(index + len(ranges)) * count : (index + len(ranges) + 1) * count]
        for plane in range(2):
            a = left[:, plane * columns : (plane + 1) * columns]
            b = right[:, plane * columns : (plane + 1) * columns]
            state[plane, first : first + count, :] = jnp.where(lane_low, a, pltpu.roll(b, half, 1))
            state[plane, second : second + count, :] = jnp.where(lane_low, pltpu.roll(a, half, 1), b)


def insert_bit(index, bit, value):
    low = index & ((1 << bit) - 1)
    return ((index >> bit) << (bit + 1)) | low | (value << bit)


def tile_at(ref, plane, index):
    return ref[plane, pl.ds(pl.multiple_of(index * TILE, TILE), TILE), :]


def in_groups(count, move):
    group = min(count, 16)

    def step(turn, carry):
        stores = []
        for inner in range(group):
            stores += move(turn * group + inner)
        for ref, plane, index, value in stores:
            ref[plane, pl.ds(pl.multiple_of(index * TILE, TILE), TILE), :] = value
        return carry

    lax.fori_loop(0, count // group, step, 0)


def permute_order(count):
    half = count // 2
    far = list(range(half, count))
    near = list(range(1, half))
    order = far[:2]
    for left, right in zip(near[1:] + near[:1], far[2:] + near[:1]):
        order += [left, right] if right in far else [left]
    return order


def row_bits(columns):
    return lax.broadcasted_iota(jnp.int32, (TILE, columns), 0)


def exchange_column_bit(state, qubit):
    rows_all, columns = state.shape[1], state.shape[2]
    half = columns // 2
    lane_low = lax.broadcasted_iota(jnp.int32, (TILE, columns), 1) < half
    sub = row_bits(columns)
    tiles = rows_all // TILE

    @pl.when(qubit >= 3)
    def _():
        def move(k):
            first = insert_bit(k, qubit - 3, 0)
            second = insert_bit(k, qubit - 3, 1)
            stores = []
            for plane in range(2):
                a = tile_at(state, plane, first)
                b = tile_at(state, plane, second)
                stores.append((state, plane, first, jnp.where(lane_low, a, pltpu.roll(b, half, 1))))
                stores.append((state, plane, second, jnp.where(lane_low, pltpu.roll(a, half, 1), b)))
            return stores

        in_groups(tiles // 2, move)

    for low_bit in range(3):

        @pl.when(qubit == low_bit)
        def _():
            distance = 1 << low_bit
            zero = ((sub >> low_bit) & 1) == 0
            keep = zero == lane_low

            def move(k):
                stores = []
                for plane in range(2):
                    a = tile_at(state, plane, k)
                    turned = pltpu.roll(a, half, 1)
                    partner = jnp.where(zero, pltpu.roll(turned, TILE - distance, 0), pltpu.roll(turned, distance, 0))
                    stores.append((state, plane, k, jnp.where(keep, a, partner)))
                return stores

            in_groups(tiles, move)


def take_out(state, sent, qubit, value):
    tiles = sent.shape[1] // TILE
    sub = row_bits(state.shape[2])

    @pl.when(qubit >= 3)
    def _():
        def move(k):
            at = insert_bit(k, qubit - 3, value)
            return [(sent, plane, k, tile_at(state, plane, at)) for plane in range(2)]

        in_groups(tiles, move)

    for low_bit in range(3):

        @pl.when(qubit == low_bit)
        def _():
            distance = 1 << low_bit
            zero = ((sub >> low_bit) & 1) == 0

            def move(k):
                stores = []
                for plane in range(2):
                    a = tile_at(state, plane, 2 * k)
                    b = tile_at(state, plane, 2 * k + 1)
                    zeros = jnp.where(zero, a, pltpu.roll(b, distance, 0))
                    ones = jnp.where(zero, pltpu.roll(a, TILE - distance, 0), b)
                    stores.append((sent, plane, k, jnp.where(value == 0, zeros, ones)))
                return stores

            in_groups(tiles, move)


def put_in(state, received, qubit, value):
    tiles = received.shape[1] // TILE
    sub = row_bits(state.shape[2])

    @pl.when(qubit >= 3)
    def _():
        def move(k):
            at = insert_bit(k, qubit - 3, value)
            return [(state, plane, at, tile_at(received, plane, k)) for plane in range(2)]

        in_groups(tiles, move)

    for low_bit in range(3):

        @pl.when(qubit == low_bit)
        def _():
            distance = 1 << low_bit
            bits = (sub >> low_bit) & 1
            zero = bits == 0
            mine = bits == value

            def move(k):
                stores = []
                for plane in range(2):
                    got = tile_at(received, plane, k)
                    a = tile_at(state, plane, 2 * k)
                    b = tile_at(state, plane, 2 * k + 1)
                    first = jnp.where(zero, got, pltpu.roll(got, distance, 0))
                    second = jnp.where(zero, pltpu.roll(got, TILE - distance, 0), got)
                    stores.append((state, plane, 2 * k, jnp.where(mine, first, a)))
                    stores.append((state, plane, 2 * k + 1, jnp.where(mine, second, b)))
                return stores

            in_groups(tiles, move)


def sums(weights):
    totals = [jnp.int32(0)]
    for weight in weights:
        totals += [total + weight for total in totals]
    return totals


def move_all(moves):
    for start in range(0, len(moves), 32):
        group = moves[start : start + 32]
        values = [tile_at(source, plane, index) for _, plane, _, source, index in group]
        for (ref, plane, index, _, _), value in zip(group, values):
            ref[plane, pl.ds(pl.multiple_of(index * TILE, TILE), TILE), :] = value


def swap_row_bits(source, state, low, high):
    sub = row_bits(state.shape[2])
    tiles = state.shape[1] // TILE
    for low_bit in range(3):

        @pl.when(low == low_bit)
        def _():
            distance = 1 << low_bit
            zero = ((sub >> low_bit) & 1) == 0

            def move(k):
                at_zero = insert_bit(k, high - 3, 0)
                at_one = insert_bit(k, high - 3, 1)
                stores = []
                for plane in range(2):
                    a = tile_at(source, plane, at_zero)
                    b = tile_at(source, plane, at_one)
                    stores.append((state, plane, at_zero, jnp.where(zero, a, pltpu.roll(b, distance, 0))))
                    stores.append((state, plane, at_one, jnp.where(zero, pltpu.roll(a, TILE - distance, 0), b)))
                return stores

            in_groups(tiles // 2, move)


class Plan:
    def __init__(self, qubits, row_count):
        self.q = [qubits[turn] for turn in range(SWAPS)]
        q0, q1, q2 = self.q
        self.bits = row_count.bit_length() - 1
        top = self.bits - 1
        self.apart = (q0 != q1) & (q0 != q2) & (q1 != q2)
        route = jnp.where(self.apart, q2, q0)
        cross = jnp.where(q1 != q0, q1, jnp.where(q0 == top, top - 1, top))
        spare = jnp.int32(top)
        for _ in range(2):
            spare = spare - ((spare == route) | (spare == cross)).astype(jnp.int32)
        target = jnp.where(self.apart, q0, spare)
        self.special = [target, route, cross]
        self.at = []
        free = jnp.int32(2)
        for bit in self.special:
            free = free + 1
            for _ in range(3):
                free = free + ((free == route) | (free == cross) | (free == target)).astype(jnp.int32)
            self.at.append(jnp.where(bit >= 3, bit, free))
        self.any_low = (route < 3) | (cross < 3) | (target < 3)
        self.target_bit, self.route_bit, self.cross_bit = self.bits - 3, self.bits - 2, self.bits - 1

    def place(self, bit):
        place = bit
        for special, at in zip(self.special, self.at):
            place = jnp.where(place == special, at, jnp.where(place == at, special, place))
        below = sum((place > at).astype(jnp.int32) for at in self.at)
        return 1 << jnp.where(bit == self.special[0], self.target_bit, place - below)

    def layout_weights(self):
        a, b, c = (at - 3 for at in self.at)
        low = jnp.minimum(jnp.minimum(a, b), c)
        high = jnp.maximum(jnp.maximum(a, b), c)
        middle = a + b + c - low - high
        rest = [insert_bit(insert_bit(insert_bit(1 << bit, low, 0), middle, 0), high, 0) for bit in range(self.bits - 6)]
        return rest + [1 << a, 1 << b, 1 << c]

    def plain_weights(self, apart):
        weights = []
        target, route = (self.route_bit, self.target_bit) if apart else (self.target_bit, self.route_bit)
        for bit in range(3, self.bits):
            below = sum((bit > at).astype(jnp.int32) for at in self.at)
            weight = 1 << (bit - 3 - below)
            for at, special in zip(self.at, (target, route, self.cross_bit)):
                weight = jnp.where(at == bit, 1 << (special - 3), weight)
            weights.append(weight)
        return weights

    def mask(self, gate, controls, me):
        q0, q1, q2 = self.q
        stage = gate // 3
        never = jnp.int32(1 << 20)
        from_core = jnp.where((me & 1) == 1, 0, never)
        from_chip = jnp.where(((me >> 1) & 1) == 1, 0, never)
        total = jnp.int32(0)
        for which in range(2):
            c = controls[which, gate]
            bit = self.place(c)
            if stage == 3:
                bit = jnp.where(self.apart & (c == q2), 1 << self.target_bit, bit)
            else:
                bit = jnp.where(self.apart & (c == q2), from_core, bit)
            bit = jnp.where(c == q1, (1 << self.cross_bit) if stage >= 2 else from_chip, bit)
            if stage:
                bit = jnp.where(c == q0, 1 << self.route_bit, bit)
                if gate % 3 == 1:
                    bit = jnp.where(c == self.q[stage - 1], 0, bit)
            else:
                bit = jnp.where(c == q0, jnp.where(self.apart, 1 << self.target_bit, from_core), bit)
            total = total | bit
        return total


def shards(state, gates, control_bits, patterns, swap_qubits):
    row_count, columns = state.shape[1], state.shape[2]
    part_count = lax.axis_size("regroup")
    swap_count = lax.axis_size("swap")
    piece_rows = row_count // part_count
    swap_levels = swap_count.bit_length() - 1
    by_permutes = part_count <= 8
    controls = control_bits.T
    half_rows, quarter_rows = row_count // 2, row_count // 4

    def array(rows):
        return VMEM((2, rows, columns), state.dtype)

    def call(kernel, name, scalars, values, outs, scratch=(), last_in_place=False):
        outs = tuple(outs)
        specs = in_vmem(len(values))
        values = list(values)
        if last_in_place:
            specs[-1] = pl.BlockSpec(memory_space=pl.ANY)
            values = resident(values[:-1]) + values[-1:]
        else:
            values = resident(values)
        return pl.pallas_call(
            kernel,
            out_shape=outs,
            in_specs=in_smem(len(scalars)) + specs,
            out_specs=tuple(in_vmem(len(outs))),
            scratch_shapes=list(scratch),
            compiler_params=limits(),
            name=name,
        )(*held_scalars(scalars), *values)

    scalars = (controls, patterns, swap_qubits)

    def give_pieces(work, pieces):
        place = lax.axis_index("regroup")
        for step in range(part_count):
            at = pl.multiple_of((place ^ step) * piece_rows, piece_rows)
            for plane in range(2):
                pieces[step][plane] = work[plane, pl.ds(at, piece_rows), :]

    def regroup(pieces):
        if not by_permutes:
            whole = pieces[0].reshape(2, part_count, piece_rows, columns)
            result = lax.all_to_all(whole, "regroup", split_axis=1, concat_axis=1, tiled=True)
            return result.reshape(2, row_count, columns)
        arrived = {0: pieces[0]}
        for step in permute_order(part_count):
            arrived[step] = lax.ppermute(pieces[step], "regroup", [(i, i ^ step) for i in range(part_count)])
        order = list(arrived)

        def assemble(*refs):
            out, semaphores = refs[part_count:]
            place = lax.axis_index("regroup")
            copies = []
            for index, step in enumerate(order):
                at = pl.multiple_of((place ^ step) * piece_rows, piece_rows)
                copies.append(pltpu.make_async_copy(refs[index], out.at[:, pl.ds(at, piece_rows), :], semaphores.at[index]))
            for copy in copies:
                copy.start()
            for copy in copies:
                copy.wait()

        return pl.pallas_call(
            assemble,
            out_shape=pltpu.HBM(state.shape, state.dtype),
            in_specs=in_vmem(part_count),
            out_specs=pl.BlockSpec(memory_space=pltpu.HBM),
            scratch_shapes=[pltpu.SemaphoreType.DMA((part_count,))],
            compiler_params=limits(),
            name="assemble",
        )(*resident(arrived[step] for step in order))

    def stage(turn, weights, current, received):
        last = turn == SWAPS

        def kernel(*refs):
            controls, pattern, qubits = refs[:3]
            high_ref, low_ref, state_in = refs[3:6]
            rest = refs[6:]
            if turn:
                got, rest = rest[0], rest[1:]
            work = rest[-1] if last and by_permutes else rest[0]
            me = lax.axis_index("swap")
            if turn:
                work[...] = state_in[...]
            else:
                pltpu.sync_copy(state_in, work)
            if turn:
                slot = 1 - ((me >> ((turn - 1) % swap_levels)) & 1)
                put_in(work, got, qubits[turn - 1], slot)
            for gate in range(3 * turn, 3 * turn + 3):
                mask = (1 << controls[0, gate]) | (1 << controls[1, gate])
                pair = turn and gate == 3 * turn + 1
                if pair:
                    qubit = qubits[turn - 1]
                    mask = mask & ~(1 << qubit)
                    exchange_column_bit(work, qubit)
                plain_gate(work, gate, (high_ref, low_ref), mask, pattern[gate], 0, half_rows)
                if pair:
                    exchange_column_bit(work, qubit)
            if not last:
                slot = 1 - ((me >> (turn % swap_levels)) & 1)
                take_out(work, rest[1], qubits[turn], slot)
            elif by_permutes:
                give_pieces(work, rest[:part_count])

        scratch = []
        if not last:
            outs = (array(row_count), array(half_rows))
        elif by_permutes:
            outs = (array(piece_rows),) * part_count
            scratch = [array(row_count)]
        else:
            outs = (array(row_count),)
        values = [*weights, current] + ([received] if turn else [])
        return call(kernel, f"stage{turn}", scalars, values, outs, scratch, last_in_place=not turn)

    def one_by_one(weights):
        current, received = state, None
        for turn in range(SWAPS):
            current, sent = stage(turn, weights, current, received)
            received = from_partner(sent, 1 << (turn % swap_levels))
        return regroup(stage(SWAPS, weights, current, received))

    def from_partner(sent, distance):
        return lax.ppermute(sent, "swap", [(i, i ^ distance) for i in range(swap_count)])

    if not (by_permutes and swap_levels == 2):
        return one_by_one(prepare(gates, (), (), lambda *refs: None)[0])

    quarter_tiles = quarter_rows // TILE

    def pack(*refs):
        qubits, state_in = refs[:2]
        messages, work = refs[2:6], refs[6]
        plan = Plan(qubits, row_count)
        me = lax.axis_index("swap")

        weights = plan.layout_weights()
        offsets = sums(weights[:-2])

        def send(source):
            for distance in (2, 3, 1, 0):
                to = me ^ distance
                base = (to & 1) * weights[-2] + (to >> 1) * weights[-1]
                move_all([(messages[distance], plane, k, source, base + at) for k, at in enumerate(offsets) for plane in range(2)])

        @pl.when(plan.any_low)
        def _():
            work[...] = state_in[...]
            for low, high in zip(plan.special, plan.at):
                swap_row_bits(work, work, low, high)
            send(work)

        @pl.when(jnp.logical_not(plan.any_low))
        def _():
            send(state_in)

    messages = call(pack, "pack", (swap_qubits,), (state,), (array(quarter_rows),) * 4, [array(row_count)])
    arrived = {0: messages[0]}
    for distance in (2, 3, 1):
        with jax.named_scope(f"from{distance}"):
            arrived[distance] = from_partner(messages[distance], distance)

    def fill(inputs, outputs):
        controls, qubits = inputs
        masks, case = outputs
        plan = Plan(qubits, row_count)
        me = lax.axis_index("swap")
        case[0] = jnp.where(qubits[0] == qubits[1], 2, jnp.where(plan.apart, 0, 1))
        for gate in range(gates.shape[1]):
            masks[gate] = plan.mask(gate, controls, me)

    outs = (SMEM((gates.shape[1],), jnp.int32), jax.ShapeDtypeStruct((1,), jnp.int32))
    weights, (masks, case) = prepare(gates, (controls, swap_qubits), outs, fill)
    layout_scalars = (masks, patterns, swap_qubits)

    def run_gates(work, plan, refs, numbers, row_base, apart=None):
        masks, pattern, weights = refs
        halves = range(0, work.shape[1], half_rows)
        for gate in numbers:
            args = (gate, weights, masks[gate], pattern[gate])
            if gate == 4:
                for start in halves:
                    pair_gate(work, *args, row_base, [(start, start + quarter_rows)], quarter_rows)
            elif gate == 7:
                for start in range(0, half_rows, quarter_rows):
                    pair_gate(work, *args, row_base, [(start, start + half_rows)], quarter_rows)
            elif gate == 10 and apart:
                eighth = quarter_rows // 2
                for start in halves:
                    ranges = [(at, at + eighth) for at in (start, start + quarter_rows)]
                    pair_gate(work, *args, row_base, ranges, eighth)
            elif gate == 10:
                qubit = jnp.where(plan.q[2] == plan.q[0], plan.route_bit, plan.cross_bit)
                exchange_column_bit(work, qubit)
                plain_gate(work, *args, row_base, half_rows)
                exchange_column_bit(work, qubit)
            else:
                plain_gate(work, *args, row_base, half_rows)

    def unpack(work, spare, plan, apart, pieces):
        weights = plan.plain_weights(apart)
        place = lax.axis_index("regroup")
        piece_tiles = piece_rows // TILE
        inner = piece_tiles.bit_length() - 1

        def give(source, weights):
            offsets = sums(weights[:inner])
            for step in permute_order(part_count) + [0]:
                to = place ^ step
                base = sum(((to >> bit) & 1) * weight for bit, weight in enumerate(weights[inner:]))
                move_all([(pieces[step], plane, k, source, base + at) for k, at in enumerate(offsets) for plane in range(2)])

        @pl.when(plan.any_low)
        def _():
            at = sums(weights)
            move_all([(spare, plane, k, work, at[k]) for k in range(row_count // TILE) for plane in range(2)])
            for low, high in zip(plan.special, plan.at):
                swap_row_bits(spare, spare, low, high)
            give(spare, [1 << bit for bit in range(len(weights))])

        @pl.when(jnp.logical_not(plan.any_low))
        def _():
            give(work, weights)

    def place_quarter(half, source, value):
        at = pl.multiple_of((source & 1) * quarter_rows, quarter_rows)
        half[:, pl.ds(at, quarter_rows), :] = value[...]

    def near(*refs):
        masks, pattern, qubits, high_ref, low_ref, own, core, work = refs
        me = lax.axis_index("swap")
        place_quarter(work, me, own)
        place_quarter(work, me ^ 1, core)
        plan = Plan(qubits, row_count)
        run_gates(work, plan, (masks, pattern, (high_ref, low_ref)), range(7), (me >> 1) * half_rows)

    values = [*weights, arrived[0], arrived[1]]
    with jax.named_scope("near"):
        near_rows = call(near, "near", layout_scalars, values, (array(half_rows),))[0]

    def merged(numbers, apart, finish):
        def kernel(*refs):
            masks, pattern, qubits, high_ref, low_ref, near_ref, third, fourth = refs[:8]
            far, work = refs[-2:]
            plan = Plan(qubits, row_count)
            me = lax.axis_index("swap")
            gate_refs = (masks, pattern, (high_ref, low_ref))
            place_quarter(far, me ^ 2, third)
            place_quarter(far, me ^ 3, fourth)
            here = pl.multiple_of((me >> 1) * half_rows, half_rows)
            there = pl.multiple_of(half_rows - here, half_rows)
            run_gates(far, plan, gate_refs, range(7), there)
            work[:, pl.ds(here, half_rows), :] = near_ref[...]
            work[:, pl.ds(there, half_rows), :] = far[...]
            run_gates(work, plan, gate_refs, numbers, 0, apart)
            finish(work, plan, refs[8:-2])

        return kernel, [*weights, near_rows, arrived[2], arrived[3]], [array(half_rows), array(row_count)]

    def all_apart():
        def finish(work, plan, refs):
            unpack(work, refs[-1], plan, True, refs[:part_count])

        kernel, values, scratch = merged(range(7, 12), True, finish)
        outs = (array(piece_rows),) * part_count
        return regroup(call(kernel, "merged", layout_scalars, values, outs, [array(row_count)] + scratch))

    def core_again():
        def slot_and_bit(plan):
            return 1 - (lax.axis_index("swap") & 1), jnp.where(plan.q[2] == plan.q[0], plan.route_bit, plan.cross_bit)

        def finish(work, plan, refs):
            refs[0][...] = work[...]
            slot, bit = slot_and_bit(plan)
            take_out(work, refs[1], bit, slot)

        kernel, values, scratch = merged(range(7, 9), False, finish)
        current, sent = call(kernel, "merged_send", layout_scalars, values, (array(row_count), array(half_rows)), scratch)
        received = from_partner(sent, 1)

        def last(*refs):
            masks, pattern, qubits, high_ref, low_ref, current_ref, got = refs[:7]
            work, spare = refs[-2:]
            plan = Plan(qubits, row_count)
            slot, bit = slot_and_bit(plan)
            work[...] = current_ref[...]
            put_in(work, got, bit, slot)
            run_gates(work, plan, (masks, pattern, (high_ref, low_ref)), range(9, 12), 0, False)
            unpack(work, spare, plan, False, refs[7:-2])

        outs = (array(piece_rows),) * part_count
        values = [*weights, current, received]
        return regroup(call(last, "last", layout_scalars, values, outs, [array(row_count)] * 2))

    return lax.switch(case[0], [all_apart, core_again, lambda: one_by_one(weights)])


def solution(mesh):
    return jax.shard_map(
        shards,
        mesh=mesh,
        in_specs=(P(None, ("swap", "regroup"), None), P(), P(), P(), P()),
        out_specs=P(None, ("swap", "regroup"), None),
        check_vma=False,
    )
```

```python
import jax
import jax.numpy as jnp
from jax import lax
from jax.experimental import pallas as pl
from jax.experimental.pallas import tpu as pltpu
from jax.sharding import PartitionSpec as P


SWAPS = 3
TILE = 8
VMEM = pltpu.VMEM
SMEM = pltpu.SMEM


def resident(values):
    return [pltpu.with_memory_space_constraint(value, VMEM) for value in values]


def held_scalars(values):
    return [pltpu.with_memory_space_constraint(value, SMEM) for value in values]


def limits():
    return pltpu.CompilerParams(vmem_limit_bytes=8 << 20)


def in_vmem(count):
    return [pl.BlockSpec(memory_space=VMEM) for _ in range(count)]


def in_smem(count):
    return [pl.BlockSpec(memory_space=SMEM) for _ in range(count)]


def prepare(gates, scalars, outs, fill):
    count, order = gates.shape[1], gates.shape[2]
    shape = VMEM((count, 2 * order, 2 * order), jnp.bfloat16)

    def kernel(*refs):
        source = refs[len(scalars)]
        high, low = refs[len(scalars) + 1 : len(scalars) + 3]
        held, semaphores = refs[-2:]
        copies = [pltpu.make_async_copy(source.at[:, gate], held.at[:, gate], semaphores.at[gate]) for gate in range(count)]
        for copy in copies:
            copy.start()
        fill(refs[: len(scalars)], refs[len(scalars) + 3 : -2])
        for gate in range(count):
            copies[gate].wait()
            real, imag = held[0, gate], held[1, gate]
            for row, col, value in ((0, 0, real), (0, 1, -imag), (1, 0, imag), (1, 1, real)):
                top = value.astype(jnp.bfloat16)
                at = (gate, slice(row * order, row * order + order), slice(col * order, col * order + order))
                high[at] = top
                low[at] = (value - top.astype(jnp.float32)).astype(jnp.bfloat16)

    high, low, *rest = pl.pallas_call(
        kernel,
        out_shape=(shape, shape, *outs),
        in_specs=in_smem(len(scalars)) + [pl.BlockSpec(memory_space=pltpu.HBM)],
        out_specs=(*in_vmem(2), *in_smem(len(outs))),
        scratch_shapes=[VMEM(gates.shape, gates.dtype), pltpu.SemaphoreType.DMA((count,))],
        compiler_params=limits(),
        name="prepare",
    )(*held_scalars(scalars), pltpu.with_memory_space_constraint(gates, pltpu.HBM))
    return (high, low), rest


def times(left, right):
    return lax.dot_general(left, right, (((1,), (1,)), ((), ())), preferred_element_type=jnp.float32)


def column_on(pattern, rows, columns):
    groups = lax.broadcasted_iota(jnp.int32, (rows, columns), 1) // (columns // 16)
    return ((pattern >> groups) & 1) == 1


def gated(both, gate, high, low, on):
    both_high = both.astype(jnp.bfloat16)
    both_low = (both - both_high.astype(jnp.float32)).astype(jnp.bfloat16)
    new = times(both_high, high[gate]) + times(both_low, high[gate]) + times(both_high, low[gate])
    return jnp.where(jnp.concatenate([on, on], axis=1), new, both)


def plain_gate(state, gate, weights, row_mask, pattern, row_base, chunk):
    rows_all, columns = state.shape[1], state.shape[2]
    rows = lax.broadcasted_iota(jnp.int32, (chunk, columns), 0) + row_base
    col_on = column_on(pattern, chunk, columns)
    for start in range(0, rows_all, chunk):
        both = jnp.concatenate([state[plane, start : start + chunk, :] for plane in range(2)], axis=1)
        on = (((rows + start) & row_mask) == row_mask) & col_on
        both = gated(both, gate, *weights, on)
        for plane in range(2):
            state[plane, start : start + chunk, :] = both[:, plane * columns : (plane + 1) * columns]


def pair_gate(state, gate, weights, row_mask, pattern, row_base, ranges, count):
    columns = state.shape[2]
    half = columns // 2
    iota = lax.broadcasted_iota(jnp.int32, (count, columns), 0) + row_base
    lane_low = lax.broadcasted_iota(jnp.int32, (count, columns), 1) < half
    col_on = column_on(pattern, count, columns)
    lowers, uppers, masks = [], [], []
    for first, second in ranges:
        lower = [state[plane, first : first + count, :] for plane in range(2)]
        upper = [state[plane, second : second + count, :] for plane in range(2)]
        lowers.append([jnp.where(lane_low, a, pltpu.roll(b, half, 1)) for a, b in zip(lower, upper)])
        uppers.append([jnp.where(lane_low, pltpu.roll(a, half, 1), b) for a, b in zip(lower, upper)])
        masks.append((((iota + first) & row_mask) == row_mask) & col_on)
    both = jnp.concatenate([jnp.concatenate(part, axis=1) for part in lowers + uppers], axis=0)
    both = gated(both, gate, *weights, jnp.concatenate(masks + masks, axis=0))
    for index, (first, second) in enumerate(ranges):
        left = both[index * count : (index + 1) * count]
        right = both[(index + len(ranges)) * count : (index + len(ranges) + 1) * count]
        for plane in range(2):
            a = left[:, plane * columns : (plane + 1) * columns]
            b = right[:, plane * columns : (plane + 1) * columns]
            state[plane, first : first + count, :] = jnp.where(lane_low, a, pltpu.roll(b, half, 1))
            state[plane, second : second + count, :] = jnp.where(lane_low, pltpu.roll(a, half, 1), b)


def insert_bit(index, bit, value):
    low = index & ((1 << bit) - 1)
    return ((index >> bit) << (bit + 1)) | low | (value << bit)


def tile_at(ref, plane, index):
    return ref[plane, pl.ds(pl.multiple_of(index * TILE, TILE), TILE), :]


def in_groups(count, move):
    group = min(count, 16)

    def step(turn, carry):
        stores = []
        for inner in range(group):
            stores += move(turn * group + inner)
        for ref, plane, index, value in stores:
            ref[plane, pl.ds(pl.multiple_of(index * TILE, TILE), TILE), :] = value
        return carry

    lax.fori_loop(0, count // group, step, 0)


def permute_order(count):
    half = count // 2
    far = list(range(half, count))
    near = list(range(1, half))
    order = far[:2]
    for left, right in zip(near[1:] + near[:1], far[2:] + near[:1]):
        order += [left, right] if right in far else [left]
    return order


def row_bits(columns):
    return lax.broadcasted_iota(jnp.int32, (TILE, columns), 0)


def exchange_column_bit(state, qubit):
    rows_all, columns = state.shape[1], state.shape[2]
    half = columns // 2
    lane_low = lax.broadcasted_iota(jnp.int32, (TILE, columns), 1) < half
    sub = row_bits(columns)
    tiles = rows_all // TILE

    @pl.when(qubit >= 3)
    def _():
        def move(k):
            first = insert_bit(k, qubit - 3, 0)
            second = insert_bit(k, qubit - 3, 1)
            stores = []
            for plane in range(2):
                a = tile_at(state, plane, first)
                b = tile_at(state, plane, second)
                stores.append((state, plane, first, jnp.where(lane_low, a, pltpu.roll(b, half, 1))))
                stores.append((state, plane, second, jnp.where(lane_low, pltpu.roll(a, half, 1), b)))
            return stores

        in_groups(tiles // 2, move)

    for low_bit in range(3):

        @pl.when(qubit == low_bit)
        def _():
            distance = 1 << low_bit
            zero = ((sub >> low_bit) & 1) == 0
            keep = zero == lane_low

            def move(k):
                stores = []
                for plane in range(2):
                    a = tile_at(state, plane, k)
                    turned = pltpu.roll(a, half, 1)
                    partner = jnp.where(zero, pltpu.roll(turned, TILE - distance, 0), pltpu.roll(turned, distance, 0))
                    stores.append((state, plane, k, jnp.where(keep, a, partner)))
                return stores

            in_groups(tiles, move)


def take_out(state, sent, qubit, value):
    tiles = sent.shape[1] // TILE
    sub = row_bits(state.shape[2])

    @pl.when(qubit >= 3)
    def _():
        def move(k):
            at = insert_bit(k, qubit - 3, value)
            return [(sent, plane, k, tile_at(state, plane, at)) for plane in range(2)]

        in_groups(tiles, move)

    for low_bit in range(3):

        @pl.when(qubit == low_bit)
        def _():
            distance = 1 << low_bit
            zero = ((sub >> low_bit) & 1) == 0

            def move(k):
                stores = []
                for plane in range(2):
                    a = tile_at(state, plane, 2 * k)
                    b = tile_at(state, plane, 2 * k + 1)
                    zeros = jnp.where(zero, a, pltpu.roll(b, distance, 0))
                    ones = jnp.where(zero, pltpu.roll(a, TILE - distance, 0), b)
                    stores.append((sent, plane, k, jnp.where(value == 0, zeros, ones)))
                return stores

            in_groups(tiles, move)


def put_in(state, received, qubit, value):
    tiles = received.shape[1] // TILE
    sub = row_bits(state.shape[2])

    @pl.when(qubit >= 3)
    def _():
        def move(k):
            at = insert_bit(k, qubit - 3, value)
            return [(state, plane, at, tile_at(received, plane, k)) for plane in range(2)]

        in_groups(tiles, move)

    for low_bit in range(3):

        @pl.when(qubit == low_bit)
        def _():
            distance = 1 << low_bit
            bits = (sub >> low_bit) & 1
            zero = bits == 0
            mine = bits == value

            def move(k):
                stores = []
                for plane in range(2):
                    got = tile_at(received, plane, k)
                    a = tile_at(state, plane, 2 * k)
                    b = tile_at(state, plane, 2 * k + 1)
                    first = jnp.where(zero, got, pltpu.roll(got, distance, 0))
                    second = jnp.where(zero, pltpu.roll(got, TILE - distance, 0), got)
                    stores.append((state, plane, 2 * k, jnp.where(mine, first, a)))
                    stores.append((state, plane, 2 * k + 1, jnp.where(mine, second, b)))
                return stores

            in_groups(tiles, move)


def sums(weights):
    totals = [jnp.int32(0)]
    for weight in weights:
        totals += [total + weight for total in totals]
    return totals


def move_all(moves):
    for start in range(0, len(moves), 32):
        group = moves[start : start + 32]
        values = [tile_at(source, plane, index) for _, plane, _, source, index in group]
        for (ref, plane, index, _, _), value in zip(group, values):
            ref[plane, pl.ds(pl.multiple_of(index * TILE, TILE), TILE), :] = value


def swap_row_bits(source, state, low, high):
    sub = row_bits(state.shape[2])
    tiles = state.shape[1] // TILE
    for low_bit in range(3):

        @pl.when(low == low_bit)
        def _():
            distance = 1 << low_bit
            zero = ((sub >> low_bit) & 1) == 0

            def move(k):
                at_zero = insert_bit(k, high - 3, 0)
                at_one = insert_bit(k, high - 3, 1)
                stores = []
                for plane in range(2):
                    a = tile_at(source, plane, at_zero)
                    b = tile_at(source, plane, at_one)
                    stores.append((state, plane, at_zero, jnp.where(zero, a, pltpu.roll(b, distance, 0))))
                    stores.append((state, plane, at_one, jnp.where(zero, pltpu.roll(a, TILE - distance, 0), b)))
                return stores

            in_groups(tiles // 2, move)


class Plan:
    def __init__(self, qubits, row_count):
        self.q = [qubits[turn] for turn in range(SWAPS)]
        q0, q1, q2 = self.q
        self.bits = row_count.bit_length() - 1
        top = self.bits - 1
        self.apart = (q0 != q1) & (q0 != q2) & (q1 != q2)
        self.joined = (q0 == q1) & (q0 != q2)
        route = jnp.where(self.apart, q2, q0)
        cross = jnp.where(q1 != q0, q1, jnp.where(q2 != q0, q2, jnp.where(q0 == top, top - 1, top)))
        spare = jnp.int32(top)
        for _ in range(2):
            spare = spare - ((spare == route) | (spare == cross)).astype(jnp.int32)
        target = jnp.where(self.apart, q0, spare)
        self.special = [target, route, cross]
        self.at = []
        free = jnp.int32(2)
        for bit in self.special:
            free = free + 1
            for _ in range(3):
                free = free + ((free == route) | (free == cross) | (free == target)).astype(jnp.int32)
            self.at.append(jnp.where(bit >= 3, bit, free))
        self.any_low = (route < 3) | (cross < 3) | (target < 3)
        self.target_bit, self.route_bit, self.cross_bit = self.bits - 3, self.bits - 2, self.bits - 1

    def place(self, bit):
        place = bit
        for special, at in zip(self.special, self.at):
            place = jnp.where(place == special, at, jnp.where(place == at, special, place))
        below = sum((place > at).astype(jnp.int32) for at in self.at)
        return 1 << jnp.where(bit == self.special[0], self.target_bit, place - below)

    def layout_weights(self):
        a, b, c = (at - 3 for at in self.at)
        low = jnp.minimum(jnp.minimum(a, b), c)
        high = jnp.maximum(jnp.maximum(a, b), c)
        middle = a + b + c - low - high
        rest = [insert_bit(insert_bit(insert_bit(1 << bit, low, 0), middle, 0), high, 0) for bit in range(self.bits - 6)]
        return rest + [1 << a, 1 << b, 1 << c]

    def plain_weights(self, case):
        weights = []
        contents = [self.target_bit, self.route_bit, self.cross_bit]
        if case == "apart":
            contents = [self.route_bit, self.target_bit, self.cross_bit]
        elif case == "joined":
            contents = [self.target_bit, self.cross_bit, self.route_bit]
        for bit in range(3, self.bits):
            below = sum((bit > at).astype(jnp.int32) for at in self.at)
            weight = 1 << (bit - 3 - below)
            for at, special in zip(self.at, contents):
                weight = jnp.where(at == bit, 1 << (special - 3), weight)
            weights.append(weight)
        return weights

    def mask(self, gate, controls, me):
        q0, q1, q2 = self.q
        stage = gate // 3
        never = jnp.int32(1 << 20)
        from_core = jnp.where((me & 1) == 1, 0, never)
        from_chip = jnp.where(((me >> 1) & 1) == 1, 0, never)
        total = jnp.int32(0)
        for which in range(2):
            c = controls[which, gate]
            bit = self.place(c)
            target, route, cross = 1 << self.target_bit, 1 << self.route_bit, 1 << self.cross_bit
            apart, joined = (target, route) if stage == 3 else (from_core, from_chip)
            bit = jnp.where(c == q2, jnp.where(self.apart, apart, jnp.where(self.joined, joined, bit)), bit)
            bit = jnp.where(c == q1, cross if stage >= 2 else from_chip, bit)
            if stage == 0:
                bit = jnp.where(c == q0, jnp.where(self.apart, target, from_core), bit)
            elif stage == 1:
                bit = jnp.where(c == q0, route, bit)
            else:
                bit = jnp.where(c == q0, jnp.where(self.joined, cross, route), bit)
            if stage and gate % 3 == 1:
                bit = jnp.where(c == self.q[stage - 1], 0, bit)
            total = total | bit
        return total


def shards(state, gates, control_bits, patterns, swap_qubits):
    row_count, columns = state.shape[1], state.shape[2]
    part_count = lax.axis_size("regroup")
    swap_count = lax.axis_size("swap")
    piece_rows = row_count // part_count
    swap_levels = swap_count.bit_length() - 1
    by_permutes = part_count <= 8
    controls = control_bits.T
    half_rows, quarter_rows = row_count // 2, row_count // 4

    def array(rows):
        return VMEM((2, rows, columns), state.dtype)

    def call(kernel, name, scalars, values, outs, scratch=(), last_in_place=False):
        outs = tuple(outs)
        specs = in_vmem(len(values))
        values = list(values)
        if last_in_place:
            specs[-1] = pl.BlockSpec(memory_space=pl.ANY)
            values = resident(values[:-1]) + values[-1:]
        else:
            values = resident(values)
        return pl.pallas_call(
            kernel,
            out_shape=outs,
            in_specs=in_smem(len(scalars)) + specs,
            out_specs=tuple(in_vmem(len(outs))),
            scratch_shapes=list(scratch),
            compiler_params=limits(),
            name=name,
        )(*held_scalars(scalars), *values)

    scalars = (controls, patterns, swap_qubits)

    def give_pieces(work, pieces):
        place = lax.axis_index("regroup")
        for step in range(part_count):
            at = pl.multiple_of((place ^ step) * piece_rows, piece_rows)
            for plane in range(2):
                pieces[step][plane] = work[plane, pl.ds(at, piece_rows), :]

    def regroup(pieces):
        if not by_permutes:
            whole = pieces[0].reshape(2, part_count, piece_rows, columns)
            result = lax.all_to_all(whole, "regroup", split_axis=1, concat_axis=1, tiled=True)
            return result.reshape(2, row_count, columns)
        arrived = {0: pieces[0]}
        for step in permute_order(part_count):
            arrived[step] = lax.ppermute(pieces[step], "regroup", [(i, i ^ step) for i in range(part_count)])
        order = list(arrived)

        def assemble(*refs):
            out, semaphores = refs[part_count:]
            place = lax.axis_index("regroup")
            copies = []
            for index, step in enumerate(order):
                at = pl.multiple_of((place ^ step) * piece_rows, piece_rows)
                copies.append(pltpu.make_async_copy(refs[index], out.at[:, pl.ds(at, piece_rows), :], semaphores.at[index]))
            for copy in copies:
                copy.start()
            for copy in copies:
                copy.wait()

        return pl.pallas_call(
            assemble,
            out_shape=pltpu.HBM(state.shape, state.dtype),
            in_specs=in_vmem(part_count),
            out_specs=pl.BlockSpec(memory_space=pltpu.HBM),
            scratch_shapes=[pltpu.SemaphoreType.DMA((part_count,))],
            compiler_params=limits(),
            name="assemble",
        )(*resident(arrived[step] for step in order))

    def stage(turn, weights, current, received):
        last = turn == SWAPS

        def kernel(*refs):
            controls, pattern, qubits = refs[:3]
            high_ref, low_ref, state_in = refs[3:6]
            rest = refs[6:]
            if turn:
                got, rest = rest[0], rest[1:]
            work = rest[-1] if last and by_permutes else rest[0]
            me = lax.axis_index("swap")
            if turn:
                work[...] = state_in[...]
            else:
                pltpu.sync_copy(state_in, work)
            if turn:
                slot = 1 - ((me >> ((turn - 1) % swap_levels)) & 1)
                put_in(work, got, qubits[turn - 1], slot)
            for gate in range(3 * turn, 3 * turn + 3):
                mask = (1 << controls[0, gate]) | (1 << controls[1, gate])
                pair = turn and gate == 3 * turn + 1
                if pair:
                    qubit = qubits[turn - 1]
                    mask = mask & ~(1 << qubit)
                    exchange_column_bit(work, qubit)
                plain_gate(work, gate, (high_ref, low_ref), mask, pattern[gate], 0, half_rows)
                if pair:
                    exchange_column_bit(work, qubit)
            if not last:
                slot = 1 - ((me >> (turn % swap_levels)) & 1)
                take_out(work, rest[1], qubits[turn], slot)
            elif by_permutes:
                give_pieces(work, rest[:part_count])

        scratch = []
        if not last:
            outs = (array(row_count), array(half_rows))
        elif by_permutes:
            outs = (array(piece_rows),) * part_count
            scratch = [array(row_count)]
        else:
            outs = (array(row_count),)
        values = [*weights, current] + ([received] if turn else [])
        return call(kernel, f"stage{turn}", scalars, values, outs, scratch, last_in_place=not turn)

    def one_by_one(weights):
        current, received = state, None
        for turn in range(SWAPS):
            current, sent = stage(turn, weights, current, received)
            received = from_partner(sent, 1 << (turn % swap_levels))
        return regroup(stage(SWAPS, weights, current, received))

    def from_partner(sent, distance):
        return lax.ppermute(sent, "swap", [(i, i ^ distance) for i in range(swap_count)])

    if not (by_permutes and swap_levels == 2):
        return one_by_one(prepare(gates, (), (), lambda *refs: None)[0])

    quarter_tiles = quarter_rows // TILE

    def pack(*refs):
        qubits, state_in = refs[:2]
        messages, work = refs[2:6], refs[6]
        plan = Plan(qubits, row_count)
        me = lax.axis_index("swap")

        weights = plan.layout_weights()
        offsets = sums(weights[:-2])

        def send(source):
            for distance in (2, 3, 1, 0):
                to = me ^ distance
                base = (to & 1) * weights[-2] + (to >> 1) * weights[-1]
                move_all([(messages[distance], plane, k, source, base + at) for k, at in enumerate(offsets) for plane in range(2)])

        @pl.when(plan.any_low)
        def _():
            work[...] = state_in[...]
            for low, high in zip(plan.special, plan.at):
                swap_row_bits(work, work, low, high)
            send(work)

        @pl.when(jnp.logical_not(plan.any_low))
        def _():
            send(state_in)

    messages = call(pack, "pack", (swap_qubits,), (state,), (array(quarter_rows),) * 4, [array(row_count)])
    arrived = {0: messages[0]}
    for distance in (2, 3, 1):
        with jax.named_scope(f"from{distance}"):
            arrived[distance] = from_partner(messages[distance], distance)

    def fill(inputs, outputs):
        controls, qubits = inputs
        masks, case = outputs
        plan = Plan(qubits, row_count)
        me = lax.axis_index("swap")
        case[0] = jnp.where(qubits[0] == qubits[1], jnp.where(plan.joined, 2, 3), jnp.where(plan.apart, 0, 1))
        for gate in range(gates.shape[1]):
            masks[gate] = plan.mask(gate, controls, me)

    outs = (SMEM((gates.shape[1],), jnp.int32), jax.ShapeDtypeStruct((1,), jnp.int32))
    weights, (masks, case) = prepare(gates, (controls, swap_qubits), outs, fill)
    layout_scalars = (masks, patterns, swap_qubits)

    def run_gates(work, plan, refs, numbers, row_base, case=None):
        masks, pattern, weights = refs
        halves = range(0, work.shape[1], half_rows)
        for gate in numbers:
            args = (gate, weights, masks[gate], pattern[gate])
            if gate == 4 or (gate == 10 and case == "joined"):
                for start in halves:
                    pair_gate(work, *args, row_base, [(start, start + quarter_rows)], quarter_rows)
            elif gate == 7:
                for start in range(0, half_rows, quarter_rows):
                    pair_gate(work, *args, row_base, [(start, start + half_rows)], quarter_rows)
            elif gate == 10 and case == "apart":
                eighth = quarter_rows // 2
                for start in halves:
                    ranges = [(at, at + eighth) for at in (start, start + quarter_rows)]
                    pair_gate(work, *args, row_base, ranges, eighth)
            elif gate == 10:
                qubit = jnp.where(plan.q[2] == plan.q[0], plan.route_bit, plan.cross_bit)
                exchange_column_bit(work, qubit)
                plain_gate(work, *args, row_base, half_rows)
                exchange_column_bit(work, qubit)
            else:
                plain_gate(work, *args, row_base, half_rows)

    def unpack(work, spare, plan, case, pieces):
        weights = plan.plain_weights(case)
        place = lax.axis_index("regroup")
        piece_tiles = piece_rows // TILE
        inner = piece_tiles.bit_length() - 1

        def give(source, weights):
            offsets = sums(weights[:inner])
            for step in permute_order(part_count) + [0]:
                to = place ^ step
                base = sum(((to >> bit) & 1) * weight for bit, weight in enumerate(weights[inner:]))
                move_all([(pieces[step], plane, k, source, base + at) for k, at in enumerate(offsets) for plane in range(2)])

        @pl.when(plan.any_low)
        def _():
            at = sums(weights)
            move_all([(spare, plane, k, work, at[k]) for k in range(row_count // TILE) for plane in range(2)])
            for low, high in zip(plan.special, plan.at):
                swap_row_bits(spare, spare, low, high)
            give(spare, [1 << bit for bit in range(len(weights))])

        @pl.when(jnp.logical_not(plan.any_low))
        def _():
            give(work, weights)

    def place_quarter(half, source, value):
        at = pl.multiple_of((source & 1) * quarter_rows, quarter_rows)
        half[:, pl.ds(at, quarter_rows), :] = value[...]

    def near(*refs):
        masks, pattern, qubits, high_ref, low_ref, own, core, work = refs
        me = lax.axis_index("swap")
        place_quarter(work, me, own)
        place_quarter(work, me ^ 1, core)
        plan = Plan(qubits, row_count)
        run_gates(work, plan, (masks, pattern, (high_ref, low_ref)), range(7), (me >> 1) * half_rows)

    values = [*weights, arrived[0], arrived[1]]
    with jax.named_scope("near"):
        near_rows = call(near, "near", layout_scalars, values, (array(half_rows),))[0]

    def merged(numbers, case, finish):
        def kernel(*refs):
            masks, pattern, qubits, high_ref, low_ref, near_ref, third, fourth = refs[:8]
            far, work = refs[-2:]
            plan = Plan(qubits, row_count)
            me = lax.axis_index("swap")
            gate_refs = (masks, pattern, (high_ref, low_ref))
            place_quarter(far, me ^ 2, third)
            place_quarter(far, me ^ 3, fourth)
            here = pl.multiple_of((me >> 1) * half_rows, half_rows)
            there = pl.multiple_of(half_rows - here, half_rows)
            run_gates(far, plan, gate_refs, range(7), there)
            work[:, pl.ds(here, half_rows), :] = near_ref[...]
            work[:, pl.ds(there, half_rows), :] = far[...]
            run_gates(work, plan, gate_refs, numbers, 0, case)
            finish(work, plan, refs[8:-2])

        return kernel, [*weights, near_rows, arrived[2], arrived[3]], [array(half_rows), array(row_count)]

    def all_apart():
        def finish(work, plan, refs):
            unpack(work, refs[-1], plan, "apart", refs[:part_count])

        kernel, values, scratch = merged(range(7, 12), "apart", finish)
        outs = (array(piece_rows),) * part_count
        return regroup(call(kernel, "merged", layout_scalars, values, outs, [array(row_count)] + scratch))

    def core_again():
        def slot_and_bit(plan):
            return 1 - (lax.axis_index("swap") & 1), jnp.where(plan.q[2] == plan.q[0], plan.route_bit, plan.cross_bit)

        def finish(work, plan, refs):
            refs[0][...] = work[...]
            slot, bit = slot_and_bit(plan)
            take_out(work, refs[1], bit, slot)

        kernel, values, scratch = merged(range(7, 9), "again", finish)
        current, sent = call(kernel, "merged_send", layout_scalars, values, (array(row_count), array(half_rows)), scratch)
        received = from_partner(sent, 1)

        def last(*refs):
            masks, pattern, qubits, high_ref, low_ref, current_ref, got = refs[:7]
            work, spare = refs[-2:]
            plan = Plan(qubits, row_count)
            slot, bit = slot_and_bit(plan)
            work[...] = current_ref[...]
            put_in(work, got, bit, slot)
            run_gates(work, plan, (masks, pattern, (high_ref, low_ref)), range(9, 12), 0, "again")
            unpack(work, spare, plan, "again", refs[7:-2])

        outs = (array(piece_rows),) * part_count
        values = [*weights, current, received]
        return regroup(call(last, "last", layout_scalars, values, outs, [array(row_count)] * 2))

    def one_qubit_twice():
        def half_of(value):
            return [(at * half_rows + value * quarter_rows, at * quarter_rows) for at in range(2)]

        def finish(work, plan, refs):
            mine = lax.axis_index("swap") & 1
            for out, value in zip(refs, (mine, 1 - mine)):
                for source, to in half_of(value):
                    out[:, to : to + quarter_rows, :] = work[:, pl.ds(pl.multiple_of(source, quarter_rows), quarter_rows), :]

        kernel, values, scratch = merged(range(7, 9), "joined", finish)
        sent = call(kernel, "merged_send", layout_scalars, values, (array(half_rows),) * 2, scratch)
        places = [(i, i & 1, i >> 1) for i in range(swap_count)]
        received = [
            lax.ppermute(sent[0], "swap", [(i, chip + 2 * core) for i, core, chip in places]),
            lax.ppermute(sent[1], "swap", [(i, chip + 2 * (1 - core)) for i, core, chip in places]),
        ]

        def last(*refs):
            masks, pattern, qubits, high_ref, low_ref = refs[:5]
            work, spare = refs[-2:]
            plan = Plan(qubits, row_count)
            chip = lax.axis_index("swap") >> 1
            for got, value in zip(refs[5:7], (chip, 1 - chip)):
                for to, source in half_of(value):
                    work[:, pl.ds(pl.multiple_of(to, quarter_rows), quarter_rows), :] = got[:, source : source + quarter_rows, :]
            run_gates(work, plan, (masks, pattern, (high_ref, low_ref)), range(9, 12), 0, "joined")
            unpack(work, spare, plan, "joined", refs[7:-2])

        outs = (array(piece_rows),) * part_count
        return regroup(call(last, "last", layout_scalars, [*weights, *received], outs, [array(row_count)] * 2))

    return lax.switch(case[0], [all_apart, core_again, one_qubit_twice, lambda: one_by_one(weights)])


def solution(mesh):
    return jax.shard_map(
        shards,
        mesh=mesh,
        in_specs=(P(None, ("swap", "regroup"), None), P(), P(), P(), P()),
        out_specs=P(None, ("swap", "regroup"), None),
        check_vma=False,
    )
```

```python
import jax
import jax.numpy as jnp
from jax import lax
from jax.experimental import pallas as pl
from jax.experimental.pallas import tpu as pltpu
from jax.sharding import PartitionSpec as P


SWAPS = 3
TILE = 8
VMEM = pltpu.VMEM
SMEM = pltpu.SMEM


def resident(values):
    return [pltpu.with_memory_space_constraint(value, VMEM) for value in values]


def held_scalars(values):
    return [pltpu.with_memory_space_constraint(value, SMEM) for value in values]


def limits():
    return pltpu.CompilerParams(vmem_limit_bytes=8 << 20)


def in_vmem(count):
    return [pl.BlockSpec(memory_space=VMEM) for _ in range(count)]


def in_smem(count):
    return [pl.BlockSpec(memory_space=SMEM) for _ in range(count)]


def prepare(gates, scalars, outs, fill):
    count, order = gates.shape[1], gates.shape[2]
    shape = VMEM((count, 2 * order, 2 * order), jnp.bfloat16)

    def kernel(*refs):
        source = refs[len(scalars)]
        high, low = refs[len(scalars) + 1 : len(scalars) + 3]
        held, semaphores = refs[-2:]
        copies = [pltpu.make_async_copy(source.at[:, gate], held.at[:, gate], semaphores.at[gate]) for gate in range(count)]
        for copy in copies:
            copy.start()
        fill(refs[: len(scalars)], refs[len(scalars) + 3 : -2])
        for gate in range(count):
            copies[gate].wait()
            real, imag = held[0, gate], held[1, gate]
            for row, col, value in ((0, 0, real), (0, 1, -imag), (1, 0, imag), (1, 1, real)):
                top = value.astype(jnp.bfloat16)
                at = (gate, slice(row * order, row * order + order), slice(col * order, col * order + order))
                high[at] = top
                low[at] = (value - top.astype(jnp.float32)).astype(jnp.bfloat16)

    high, low, *rest = pl.pallas_call(
        kernel,
        out_shape=(shape, shape, *outs),
        in_specs=in_smem(len(scalars)) + [pl.BlockSpec(memory_space=pltpu.HBM)],
        out_specs=(*in_vmem(2), *in_smem(len(outs))),
        scratch_shapes=[VMEM(gates.shape, gates.dtype), pltpu.SemaphoreType.DMA((count,))],
        compiler_params=limits(),
        name="prepare",
    )(*held_scalars(scalars), pltpu.with_memory_space_constraint(gates, pltpu.HBM))
    return (high, low), rest


def times(left, right):
    return lax.dot_general(left, right, (((1,), (1,)), ((), ())), preferred_element_type=jnp.float32)


def column_on(pattern, rows, columns):
    groups = lax.broadcasted_iota(jnp.int32, (rows, columns), 1) // (columns // 16)
    return ((pattern >> groups) & 1) == 1


def gated(both, gate, high, low, on):
    both_high = both.astype(jnp.bfloat16)
    both_low = (both - both_high.astype(jnp.float32)).astype(jnp.bfloat16)
    new = times(both_high, high[gate]) + times(both_low, high[gate]) + times(both_high, low[gate])
    return jnp.where(jnp.concatenate([on, on], axis=1), new, both)


def plain_gate(state, gate, weights, row_mask, pattern, row_base, chunk):
    rows_all, columns = state.shape[1], state.shape[2]
    rows = lax.broadcasted_iota(jnp.int32, (chunk, columns), 0) + row_base
    col_on = column_on(pattern, chunk, columns)
    for start in range(0, rows_all, chunk):
        both = jnp.concatenate([state[plane, start : start + chunk, :] for plane in range(2)], axis=1)
        on = (((rows + start) & row_mask) == row_mask) & col_on
        both = gated(both, gate, *weights, on)
        for plane in range(2):
            state[plane, start : start + chunk, :] = both[:, plane * columns : (plane + 1) * columns]


def pair_gate(state, gate, weights, row_mask, pattern, row_base, ranges, count):
    columns = state.shape[2]
    half = columns // 2
    iota = lax.broadcasted_iota(jnp.int32, (count, columns), 0) + row_base
    lane_low = lax.broadcasted_iota(jnp.int32, (count, columns), 1) < half
    col_on = column_on(pattern, count, columns)
    lowers, uppers, masks = [], [], []
    for first, second in ranges:
        lower = [state[plane, first : first + count, :] for plane in range(2)]
        upper = [state[plane, second : second + count, :] for plane in range(2)]
        lowers.append([jnp.where(lane_low, a, pltpu.roll(b, half, 1)) for a, b in zip(lower, upper)])
        uppers.append([jnp.where(lane_low, pltpu.roll(a, half, 1), b) for a, b in zip(lower, upper)])
        masks.append((((iota + first) & row_mask) == row_mask) & col_on)
    both = jnp.concatenate([jnp.concatenate(part, axis=1) for part in lowers + uppers], axis=0)
    both = gated(both, gate, *weights, jnp.concatenate(masks + masks, axis=0))
    for index, (first, second) in enumerate(ranges):
        left = both[index * count : (index + 1) * count]
        right = both[(index + len(ranges)) * count : (index + len(ranges) + 1) * count]
        for plane in range(2):
            a = left[:, plane * columns : (plane + 1) * columns]
            b = right[:, plane * columns : (plane + 1) * columns]
            state[plane, first : first + count, :] = jnp.where(lane_low, a, pltpu.roll(b, half, 1))
            state[plane, second : second + count, :] = jnp.where(lane_low, pltpu.roll(a, half, 1), b)


def insert_bit(index, bit, value):
    low = index & ((1 << bit) - 1)
    return ((index >> bit) << (bit + 1)) | low | (value << bit)


def tile_at(ref, plane, index):
    return ref[plane, pl.ds(pl.multiple_of(index * TILE, TILE), TILE), :]


def in_groups(count, move):
    group = min(count, 16)

    def step(turn, carry):
        stores = []
        for inner in range(group):
            stores += move(turn * group + inner)
        for ref, plane, index, value in stores:
            ref[plane, pl.ds(pl.multiple_of(index * TILE, TILE), TILE), :] = value
        return carry

    lax.fori_loop(0, count // group, step, 0)


def permute_order(count):
    half = count // 2
    far = list(range(half, count))
    near = list(range(1, half))
    order = far[:2]
    for left, right in zip(near[1:] + near[:1], far[2:] + near[:1]):
        order += [left, right] if right in far else [left]
    return order


def row_bits(columns):
    return lax.broadcasted_iota(jnp.int32, (TILE, columns), 0)


def exchange_column_bit(state, qubit):
    rows_all, columns = state.shape[1], state.shape[2]
    half = columns // 2
    lane_low = lax.broadcasted_iota(jnp.int32, (TILE, columns), 1) < half
    sub = row_bits(columns)
    tiles = rows_all // TILE

    @pl.when(qubit >= 3)
    def _():
        def move(k):
            first = insert_bit(k, qubit - 3, 0)
            second = insert_bit(k, qubit - 3, 1)
            stores = []
            for plane in range(2):
                a = tile_at(state, plane, first)
                b = tile_at(state, plane, second)
                stores.append((state, plane, first, jnp.where(lane_low, a, pltpu.roll(b, half, 1))))
                stores.append((state, plane, second, jnp.where(lane_low, pltpu.roll(a, half, 1), b)))
            return stores

        in_groups(tiles // 2, move)

    for low_bit in range(3):

        @pl.when(qubit == low_bit)
        def _():
            distance = 1 << low_bit
            zero = ((sub >> low_bit) & 1) == 0
            keep = zero == lane_low

            def move(k):
                stores = []
                for plane in range(2):
                    a = tile_at(state, plane, k)
                    turned = pltpu.roll(a, half, 1)
                    partner = jnp.where(zero, pltpu.roll(turned, TILE - distance, 0), pltpu.roll(turned, distance, 0))
                    stores.append((state, plane, k, jnp.where(keep, a, partner)))
                return stores

            in_groups(tiles, move)


def take_out(state, sent, qubit, value):
    tiles = sent.shape[1] // TILE
    sub = row_bits(state.shape[2])

    @pl.when(qubit >= 3)
    def _():
        def move(k):
            at = insert_bit(k, qubit - 3, value)
            return [(sent, plane, k, tile_at(state, plane, at)) for plane in range(2)]

        in_groups(tiles, move)

    for low_bit in range(3):

        @pl.when(qubit == low_bit)
        def _():
            distance = 1 << low_bit
            zero = ((sub >> low_bit) & 1) == 0

            def move(k):
                stores = []
                for plane in range(2):
                    a = tile_at(state, plane, 2 * k)
                    b = tile_at(state, plane, 2 * k + 1)
                    zeros = jnp.where(zero, a, pltpu.roll(b, distance, 0))
                    ones = jnp.where(zero, pltpu.roll(a, TILE - distance, 0), b)
                    stores.append((sent, plane, k, jnp.where(value == 0, zeros, ones)))
                return stores

            in_groups(tiles, move)


def put_in(state, received, qubit, value):
    tiles = received.shape[1] // TILE
    sub = row_bits(state.shape[2])

    @pl.when(qubit >= 3)
    def _():
        def move(k):
            at = insert_bit(k, qubit - 3, value)
            return [(state, plane, at, tile_at(received, plane, k)) for plane in range(2)]

        in_groups(tiles, move)

    for low_bit in range(3):

        @pl.when(qubit == low_bit)
        def _():
            distance = 1 << low_bit
            bits = (sub >> low_bit) & 1
            zero = bits == 0
            mine = bits == value

            def move(k):
                stores = []
                for plane in range(2):
                    got = tile_at(received, plane, k)
                    a = tile_at(state, plane, 2 * k)
                    b = tile_at(state, plane, 2 * k + 1)
                    first = jnp.where(zero, got, pltpu.roll(got, distance, 0))
                    second = jnp.where(zero, pltpu.roll(got, TILE - distance, 0), got)
                    stores.append((state, plane, 2 * k, jnp.where(mine, first, a)))
                    stores.append((state, plane, 2 * k + 1, jnp.where(mine, second, b)))
                return stores

            in_groups(tiles, move)


def sums(weights):
    totals = [jnp.int32(0)]
    for weight in weights:
        totals += [total + weight for total in totals]
    return totals


def move_all(moves):
    for start in range(0, len(moves), 32):
        group = moves[start : start + 32]
        values = [tile_at(source, plane, index) for _, plane, _, source, index in group]
        for (ref, plane, index, _, _), value in zip(group, values):
            ref[plane, pl.ds(pl.multiple_of(index * TILE, TILE), TILE), :] = value


def swap_row_bits(source, state, low, high):
    sub = row_bits(state.shape[2])
    tiles = state.shape[1] // TILE
    for low_bit in range(3):

        @pl.when(low == low_bit)
        def _():
            distance = 1 << low_bit
            zero = ((sub >> low_bit) & 1) == 0

            def move(k):
                at_zero = insert_bit(k, high - 3, 0)
                at_one = insert_bit(k, high - 3, 1)
                stores = []
                for plane in range(2):
                    a = tile_at(source, plane, at_zero)
                    b = tile_at(source, plane, at_one)
                    stores.append((state, plane, at_zero, jnp.where(zero, a, pltpu.roll(b, distance, 0))))
                    stores.append((state, plane, at_one, jnp.where(zero, pltpu.roll(a, TILE - distance, 0), b)))
                return stores

            in_groups(tiles // 2, move)


class Plan:
    def __init__(self, qubits, row_count):
        self.q = [qubits[turn] for turn in range(SWAPS)]
        q0, q1, q2 = self.q
        self.bits = row_count.bit_length() - 1
        top = self.bits - 1
        self.apart = (q0 != q1) & (q0 != q2) & (q1 != q2)
        self.joined = (q0 == q1) & (q0 != q2)
        route = jnp.where(self.apart, q2, q0)
        cross = jnp.where(q1 != q0, q1, jnp.where(q2 != q0, q2, jnp.where(q0 == top, top - 1, top)))
        spare = jnp.int32(top)
        for _ in range(2):
            spare = spare - ((spare == route) | (spare == cross)).astype(jnp.int32)
        target = jnp.where(self.apart, q0, spare)
        self.special = [target, route, cross]
        self.at = []
        free = jnp.int32(2)
        for bit in self.special:
            free = free + 1
            for _ in range(3):
                free = free + ((free == route) | (free == cross) | (free == target)).astype(jnp.int32)
            self.at.append(jnp.where(bit >= 3, bit, free))
        self.any_low = (route < 3) | (cross < 3) | (target < 3)
        self.target_bit, self.route_bit, self.cross_bit = self.bits - 3, self.bits - 2, self.bits - 1

    def place(self, bit):
        place = bit
        for special, at in zip(self.special, self.at):
            place = jnp.where(place == special, at, jnp.where(place == at, special, place))
        below = sum((place > at).astype(jnp.int32) for at in self.at)
        return 1 << jnp.where(bit == self.special[0], self.target_bit, place - below)

    def layout_weights(self):
        a, b, c = (at - 3 for at in self.at)
        low = jnp.minimum(jnp.minimum(a, b), c)
        high = jnp.maximum(jnp.maximum(a, b), c)
        middle = a + b + c - low - high
        rest = [insert_bit(insert_bit(insert_bit(1 << bit, low, 0), middle, 0), high, 0) for bit in range(self.bits - 6)]
        return rest + [1 << a, 1 << b, 1 << c]

    def plain_weights(self, case):
        weights = []
        contents = [self.target_bit, self.route_bit, self.cross_bit]
        if case == "apart":
            contents = [self.route_bit, self.target_bit, self.cross_bit]
        elif case == "joined":
            contents = [self.target_bit, self.cross_bit, self.route_bit]
        for bit in range(3, self.bits):
            below = sum((bit > at).astype(jnp.int32) for at in self.at)
            weight = 1 << (bit - 3 - below)
            for at, special in zip(self.at, contents):
                weight = jnp.where(at == bit, 1 << (special - 3), weight)
            weights.append(weight)
        return weights

    def mask(self, gate, controls, me):
        q0, q1, q2 = self.q
        stage = gate // 3
        never = jnp.int32(1 << 20)
        from_core = jnp.where((me & 1) == 1, 0, never)
        from_chip = jnp.where(((me >> 1) & 1) == 1, 0, never)
        total = jnp.int32(0)
        for which in range(2):
            c = controls[which, gate]
            bit = self.place(c)
            target, route, cross = 1 << self.target_bit, 1 << self.route_bit, 1 << self.cross_bit
            apart, joined = (target, route) if stage == 3 else (from_core, from_chip)
            bit = jnp.where(c == q2, jnp.where(self.apart, apart, jnp.where(self.joined, joined, bit)), bit)
            bit = jnp.where(c == q1, cross if stage >= 2 else from_chip, bit)
            if stage == 0:
                bit = jnp.where(c == q0, jnp.where(self.apart, target, from_core), bit)
            elif stage == 1:
                bit = jnp.where(c == q0, route, bit)
            else:
                bit = jnp.where(c == q0, jnp.where(self.joined, cross, route), bit)
            if stage and gate % 3 == 1:
                bit = jnp.where(c == self.q[stage - 1], 0, bit)
            total = total | bit
        return total


def shards(state, gates, control_bits, patterns, swap_qubits):
    row_count, columns = state.shape[1], state.shape[2]
    part_count = lax.axis_size("regroup")
    swap_count = lax.axis_size("swap")
    piece_rows = row_count // part_count
    swap_levels = swap_count.bit_length() - 1
    by_permutes = part_count <= 8
    controls = control_bits.T
    half_rows, quarter_rows = row_count // 2, row_count // 4

    def array(rows):
        return VMEM((2, rows, columns), state.dtype)

    def call(kernel, name, scalars, values, outs, scratch=(), last_in_place=False):
        outs = tuple(outs)
        specs = in_vmem(len(values))
        values = list(values)
        if last_in_place:
            specs[-1] = pl.BlockSpec(memory_space=pl.ANY)
            values = resident(values[:-1]) + values[-1:]
        else:
            values = resident(values)
        return pl.pallas_call(
            kernel,
            out_shape=outs,
            in_specs=in_smem(len(scalars)) + specs,
            out_specs=tuple(in_vmem(len(outs))),
            scratch_shapes=list(scratch),
            compiler_params=limits(),
            name=name,
        )(*held_scalars(scalars), *values)

    scalars = (controls, patterns, swap_qubits)

    def give_pieces(work, pieces):
        place = lax.axis_index("regroup")
        for step in range(part_count):
            at = pl.multiple_of((place ^ step) * piece_rows, piece_rows)
            for plane in range(2):
                pieces[step][plane] = work[plane, pl.ds(at, piece_rows), :]

    def regroup(pieces):
        if not by_permutes:
            whole = pieces[0].reshape(2, part_count, piece_rows, columns)
            result = lax.all_to_all(whole, "regroup", split_axis=1, concat_axis=1, tiled=True)
            return result.reshape(2, row_count, columns)
        arrived = {0: pieces[0]}
        for step in permute_order(part_count):
            arrived[step] = lax.ppermute(pieces[step], "regroup", [(i, i ^ step) for i in range(part_count)])
        order = list(arrived)

        def assemble(*refs):
            out, semaphores = refs[part_count:]
            place = lax.axis_index("regroup")
            copies = []
            for index, step in enumerate(order):
                at = pl.multiple_of((place ^ step) * piece_rows, piece_rows)
                copies.append(pltpu.make_async_copy(refs[index], out.at[:, pl.ds(at, piece_rows), :], semaphores.at[index]))
            for copy in copies:
                copy.start()
            for copy in copies:
                copy.wait()

        return pl.pallas_call(
            assemble,
            out_shape=pltpu.HBM(state.shape, state.dtype),
            in_specs=in_vmem(part_count),
            out_specs=pl.BlockSpec(memory_space=pltpu.HBM),
            scratch_shapes=[pltpu.SemaphoreType.DMA((part_count,))],
            compiler_params=limits(),
            name="assemble",
        )(*resident(arrived[step] for step in order))

    def stage(turn, weights, current, received):
        last = turn == SWAPS

        def kernel(*refs):
            controls, pattern, qubits = refs[:3]
            high_ref, low_ref, state_in = refs[3:6]
            rest = refs[6:]
            if turn:
                got, rest = rest[0], rest[1:]
            work = rest[-1] if last and by_permutes else rest[0]
            me = lax.axis_index("swap")
            if turn:
                work[...] = state_in[...]
            else:
                pltpu.sync_copy(state_in, work)
            if turn:
                slot = 1 - ((me >> ((turn - 1) % swap_levels)) & 1)
                put_in(work, got, qubits[turn - 1], slot)
            for gate in range(3 * turn, 3 * turn + 3):
                mask = (1 << controls[0, gate]) | (1 << controls[1, gate])
                pair = turn and gate == 3 * turn + 1
                if pair:
                    qubit = qubits[turn - 1]
                    mask = mask & ~(1 << qubit)
                    exchange_column_bit(work, qubit)
                plain_gate(work, gate, (high_ref, low_ref), mask, pattern[gate], 0, half_rows)
                if pair:
                    exchange_column_bit(work, qubit)
            if not last:
                slot = 1 - ((me >> (turn % swap_levels)) & 1)
                take_out(work, rest[1], qubits[turn], slot)
            elif by_permutes:
                give_pieces(work, rest[:part_count])

        scratch = []
        if not last:
            outs = (array(row_count), array(half_rows))
        elif by_permutes:
            outs = (array(piece_rows),) * part_count
            scratch = [array(row_count)]
        else:
            outs = (array(row_count),)
        values = [*weights, current] + ([received] if turn else [])
        return call(kernel, f"stage{turn}", scalars, values, outs, scratch, last_in_place=not turn)

    def one_by_one(weights):
        current, received = state, None
        for turn in range(SWAPS):
            current, sent = stage(turn, weights, current, received)
            received = from_partner(sent, 1 << (turn % swap_levels))
        return regroup(stage(SWAPS, weights, current, received))

    def from_partner(sent, distance):
        return lax.ppermute(sent, "swap", [(i, i ^ distance) for i in range(swap_count)])

    if not (by_permutes and swap_levels == 2):
        return one_by_one(prepare(gates, (), (), lambda *refs: None)[0])

    quarter_tiles = quarter_rows // TILE

    def pack(qubits_in, state_in, *refs):
        messages = refs[:4]
        held, work, qubits, state_done, qubits_done = refs[4:]
        state_copy = pltpu.make_async_copy(state_in, held, state_done)
        qubits_copy = pltpu.make_async_copy(qubits_in, qubits, qubits_done)
        qubits_copy.start()
        state_copy.start()
        qubits_copy.wait()
        plan = Plan(qubits, row_count)
        me = lax.axis_index("swap")
        weights = plan.layout_weights()
        offsets = sums(weights[:-2])

        def send(source):
            for distance in (2, 3, 1, 0):
                to = me ^ distance
                base = (to & 1) * weights[-2] + (to >> 1) * weights[-1]
                move_all([(messages[distance], plane, k, source, base + at) for k, at in enumerate(offsets) for plane in range(2)])

        state_copy.wait()

        @pl.when(plan.any_low)
        def _():
            work[...] = held[...]
            for low, high in zip(plan.special, plan.at):
                swap_row_bits(work, work, low, high)
            send(work)

        @pl.when(jnp.logical_not(plan.any_low))
        def _():
            send(held)

    messages = pl.pallas_call(
        pack,
        out_shape=(array(quarter_rows),) * 4,
        in_specs=[pl.BlockSpec(memory_space=pltpu.HBM)] * 2,
        out_specs=tuple(in_vmem(4)),
        scratch_shapes=[array(row_count)] * 2
        + [SMEM(swap_qubits.shape, swap_qubits.dtype), pltpu.SemaphoreType.DMA, pltpu.SemaphoreType.DMA],
        compiler_params=limits(),
        name="pack",
    )(*(pltpu.with_memory_space_constraint(value, pltpu.HBM) for value in (swap_qubits, state)))
    arrived = {0: messages[0]}
    for distance in (2, 3, 1):
        with jax.named_scope(f"from{distance}"):
            arrived[distance] = from_partner(messages[distance], distance)

    def fill(inputs, outputs):
        controls, qubits = inputs
        masks, case = outputs
        plan = Plan(qubits, row_count)
        me = lax.axis_index("swap")
        case[0] = jnp.where(qubits[0] == qubits[1], jnp.where(plan.joined, 2, 3), jnp.where(plan.apart, 0, 1))
        for gate in range(gates.shape[1]):
            masks[gate] = plan.mask(gate, controls, me)

    outs = (SMEM((gates.shape[1],), jnp.int32), jax.ShapeDtypeStruct((1,), jnp.int32))
    weights, (masks, case) = prepare(gates, (controls, swap_qubits), outs, fill)
    layout_scalars = (masks, patterns, swap_qubits)

    def run_gates(work, plan, refs, numbers, row_base, case=None):
        masks, pattern, weights = refs
        halves = range(0, work.shape[1], half_rows)
        for gate in numbers:
            args = (gate, weights, masks[gate], pattern[gate])
            if gate == 4 or (gate == 10 and case == "joined"):
                for start in halves:
                    pair_gate(work, *args, row_base, [(start, start + quarter_rows)], quarter_rows)
            elif gate == 7:
                for start in range(0, half_rows, quarter_rows):
                    pair_gate(work, *args, row_base, [(start, start + half_rows)], quarter_rows)
            elif gate == 10 and case == "apart":
                eighth = quarter_rows // 2
                for start in halves:
                    ranges = [(at, at + eighth) for at in (start, start + quarter_rows)]
                    pair_gate(work, *args, row_base, ranges, eighth)
            elif gate == 10:
                qubit = jnp.where(plan.q[2] == plan.q[0], plan.route_bit, plan.cross_bit)
                exchange_column_bit(work, qubit)
                plain_gate(work, *args, row_base, half_rows)
                exchange_column_bit(work, qubit)
            else:
                plain_gate(work, *args, row_base, half_rows)

    def unpack(work, spare, plan, case, pieces):
        weights = plan.plain_weights(case)
        place = lax.axis_index("regroup")
        piece_tiles = piece_rows // TILE
        inner = piece_tiles.bit_length() - 1

        def give(source, weights):
            offsets = sums(weights[:inner])
            for step in permute_order(part_count) + [0]:
                to = place ^ step
                base = sum(((to >> bit) & 1) * weight for bit, weight in enumerate(weights[inner:]))
                move_all([(pieces[step], plane, k, source, base + at) for k, at in enumerate(offsets) for plane in range(2)])

        @pl.when(plan.any_low)
        def _():
            at = sums(weights)
            move_all([(spare, plane, k, work, at[k]) for k in range(row_count // TILE) for plane in range(2)])
            for low, high in zip(plan.special, plan.at):
                swap_row_bits(spare, spare, low, high)
            give(spare, [1 << bit for bit in range(len(weights))])

        @pl.when(jnp.logical_not(plan.any_low))
        def _():
            give(work, weights)

    def place_quarter(half, source, value):
        at = pl.multiple_of((source & 1) * quarter_rows, quarter_rows)
        half[:, pl.ds(at, quarter_rows), :] = value[...]

    def near(*refs):
        masks, pattern, qubits, high_ref, low_ref, own, core, work = refs
        me = lax.axis_index("swap")
        place_quarter(work, me, own)
        place_quarter(work, me ^ 1, core)
        plan = Plan(qubits, row_count)
        run_gates(work, plan, (masks, pattern, (high_ref, low_ref)), range(7), (me >> 1) * half_rows)

    values = [*weights, arrived[0], arrived[1]]
    with jax.named_scope("near"):
        near_rows = call(near, "near", layout_scalars, values, (array(half_rows),))[0]

    def merged(numbers, case, finish):
        def kernel(*refs):
            masks, pattern, qubits, high_ref, low_ref, near_ref, third, fourth = refs[:8]
            far, work = refs[-2:]
            plan = Plan(qubits, row_count)
            me = lax.axis_index("swap")
            gate_refs = (masks, pattern, (high_ref, low_ref))
            place_quarter(far, me ^ 2, third)
            place_quarter(far, me ^ 3, fourth)
            here = pl.multiple_of((me >> 1) * half_rows, half_rows)
            there = pl.multiple_of(half_rows - here, half_rows)
            run_gates(far, plan, gate_refs, range(7), there)
            work[:, pl.ds(here, half_rows), :] = near_ref[...]
            work[:, pl.ds(there, half_rows), :] = far[...]
            run_gates(work, plan, gate_refs, numbers, 0, case)
            finish(work, plan, refs[8:-2])

        return kernel, [*weights, near_rows, arrived[2], arrived[3]], [array(half_rows), array(row_count)]

    def all_apart():
        def finish(work, plan, refs):
            unpack(work, refs[-1], plan, "apart", refs[:part_count])

        kernel, values, scratch = merged(range(7, 12), "apart", finish)
        outs = (array(piece_rows),) * part_count
        return regroup(call(kernel, "merged", layout_scalars, values, outs, [array(row_count)] + scratch))

    def core_again():
        def slot_and_bit(plan):
            return 1 - (lax.axis_index("swap") & 1), jnp.where(plan.q[2] == plan.q[0], plan.route_bit, plan.cross_bit)

        def finish(work, plan, refs):
            refs[0][...] = work[...]
            slot, bit = slot_and_bit(plan)
            take_out(work, refs[1], bit, slot)

        kernel, values, scratch = merged(range(7, 9), "again", finish)
        current, sent = call(kernel, "merged_send", layout_scalars, values, (array(row_count), array(half_rows)), scratch)
        received = from_partner(sent, 1)

        def last(*refs):
            masks, pattern, qubits, high_ref, low_ref, current_ref, got = refs[:7]
            work, spare = refs[-2:]
            plan = Plan(qubits, row_count)
            slot, bit = slot_and_bit(plan)
            work[...] = current_ref[...]
            put_in(work, got, bit, slot)
            run_gates(work, plan, (masks, pattern, (high_ref, low_ref)), range(9, 12), 0, "again")
            unpack(work, spare, plan, "again", refs[7:-2])

        outs = (array(piece_rows),) * part_count
        values = [*weights, current, received]
        return regroup(call(last, "last", layout_scalars, values, outs, [array(row_count)] * 2))

    def one_qubit_twice():
        def half_of(value):
            return [(at * half_rows + value * quarter_rows, at * quarter_rows) for at in range(2)]

        def finish(work, plan, refs):
            mine = lax.axis_index("swap") & 1
            for out, value in zip(refs, (mine, 1 - mine)):
                for source, to in half_of(value):
                    out[:, to : to + quarter_rows, :] = work[:, pl.ds(pl.multiple_of(source, quarter_rows), quarter_rows), :]

        kernel, values, scratch = merged(range(7, 9), "joined", finish)
        sent = call(kernel, "merged_send", layout_scalars, values, (array(half_rows),) * 2, scratch)
        places = [(i, i & 1, i >> 1) for i in range(swap_count)]
        received = [
            lax.ppermute(sent[0], "swap", [(i, chip + 2 * core) for i, core, chip in places]),
            lax.ppermute(sent[1], "swap", [(i, chip + 2 * (1 - core)) for i, core, chip in places]),
        ]

        def last(*refs):
            masks, pattern, qubits, high_ref, low_ref = refs[:5]
            work, spare = refs[-2:]
            plan = Plan(qubits, row_count)
            chip = lax.axis_index("swap") >> 1
            for got, value in zip(refs[5:7], (chip, 1 - chip)):
                for to, source in half_of(value):
                    work[:, pl.ds(pl.multiple_of(to, quarter_rows), quarter_rows), :] = got[:, source : source + quarter_rows, :]
            run_gates(work, plan, (masks, pattern, (high_ref, low_ref)), range(9, 12), 0, "joined")
            unpack(work, spare, plan, "joined", refs[7:-2])

        outs = (array(piece_rows),) * part_count
        return regroup(call(last, "last", layout_scalars, [*weights, *received], outs, [array(row_count)] * 2))

    return lax.switch(case[0], [all_apart, core_again, one_qubit_twice, lambda: one_by_one(weights)])


def solution(mesh):
    return jax.shard_map(
        shards,
        mesh=mesh,
        in_specs=(P(None, ("swap", "regroup"), None), P(), P(), P(), P()),
        out_specs=P(None, ("swap", "regroup"), None),
        check_vma=False,
    )
```
